128 devices in a mesh: gx: 16 (over y_lo, z, core), gy: 8 (over x, y_hi).
Axes of the slice: x: 4, y: 4 (y_hi: 2, y_lo: 2; y = y_hi * 2 + y_lo), z: 4, core: 2. Of those that a mesh axis runs over, the one named last changes fastest.
Arguments:
- mass: float32 [5, 512, 2048], P(None, 'gy', 'gx'), may hold values from 0.05 to 1
- tracer: float32 [5, 7, 512, 2048], P(None, None, 'gy', 'gx'), may hold values from -4 to 4
- uvel: float32 [512, 2048], P('gy', 'gx'), may hold values from -0.45 to 0.45
- vvel: float32 [512, 2048], P('gy', 'gx'), may hold values from -0.45 to 0.45
- case_east: int32 [512, 2048], P('gy', 'gx'), may hold values from 0 to 2
- case_north: int32 [512, 2048], P('gy', 'gx'), may hold values from 0 to 2
- ice_blocks: int32 [16, 64], P('gy', 'gx'), may hold values 0 or 1
Outputs:
- mass_out: float32 [5, 512, 2048], P(None, 'gy', 'gx')
- tracer_out: float32 [5, 7, 512, 2048], P(None, None, 'gy', 'gx')
The draws below stay inside these ranges and needn't reach their ends.
Inputs may be any that keep to these rules, and one draw needn't show every extreme that they name: `case_east`: 0 means no corner triangle, 1 the lower corner, 2 the upper corner. `case_north`: 0 means no corner triangle, 1 the western corner, 2 the eastern corner.
All inputs are finite; a program needn't handle non-finite values. No bound on the sum of `ice_blocks` on one device may be relied on, other than what follows from the above.
Results may differ from the reference program's by a relative error of at most 0.0003.
Values sent between devices are 32-bit elements; how exact they have to be, the bound alone decides.
A program may use at most 128 MiB of HBM per device.

```python
import jax
import jax.numpy as jnp
from jax import lax

NCAT = 5
NTRC = 7
BS = 32
STEPS = 2
NX = 2048
NY = 512


def place_ends(values, own_key, least, top_value):
    dims = values.shape
    place = [jax.random.randint(jax.random.fold_in(own_key, axis), (), 0, dims[axis]) for axis in range(len(dims))]
    values = values.at[tuple(place)].set(least)
    longest = dims.index(max(dims))
    place[longest] = (place[longest] + 1) % dims[longest]
    return values.at[tuple(place)].set(top_value)


def levels(own_key, shape, pieces, least, largest):
    level = 1.0
    for dim, blocks in pieces:
        heights = jax.random.uniform(jax.random.fold_in(jax.random.fold_in(own_key, 6), dim), (blocks,), jnp.float32, least / len(pieces), largest / len(pieces))
        level = level * jnp.repeat(jnp.exp(heights), shape[dim] // blocks).reshape((-1,) + (1,) * (len(shape) - 1 - dim))
    return level


def scatter_about(key, shape, deviation, bound, cuts=(), dtype=jnp.bfloat16):
    entries = deviation * jax.random.normal(key, shape, jnp.float32)
    if cuts:
        entries = entries * levels(key, shape, cuts, -0.22, 0.18)
    return jnp.clip(entries, -bound, bound).astype(dtype)


def setup_inputs(seed: int = 0) -> dict:
    arg_keys = jax.random.split(jax.random.key(seed), 8)
    mass = jnp.clip(0.05 + 0.95 * jax.random.uniform(arg_keys[0], (NCAT, NY, NX), jnp.float32) ** levels(arg_keys[0], (NCAT, NY, NX), ((1, 8), (2, 16)), -0.2, 0.2), 0.05, 1.0)
    tracer = scatter_about(arg_keys[1], (NCAT, NTRC, NY, NX), 1.0, 4.0, ((2, 8), (3, 16)), jnp.float32)
    uvel = jnp.clip(jax.random.uniform(arg_keys[2], (NY, NX), jnp.float32, -0.45, 0.45) * levels(arg_keys[2], (NY, NX), ((0, 8), (1, 16)), -0.4, 0.0), -0.45, 0.45)
    vvel = jnp.clip(jax.random.uniform(arg_keys[3], (NY, NX), jnp.float32, -0.45, 0.45) * levels(arg_keys[3], (NY, NX), ((0, 8), (1, 16)), -0.4, 0.0), -0.45, 0.45)
    case_east = place_ends(jax.random.randint(arg_keys[4], (NY, NX), 0, 3), jax.random.fold_in(arg_keys[4], 1), 0, 2).astype(jnp.int32)
    case_north = place_ends(jax.random.randint(arg_keys[5], (NY, NX), 0, 3), jax.random.fold_in(arg_keys[5], 1), 0, 2).astype(jnp.int32)
    ice_blocks = place_ends((jax.random.randint(arg_keys[6], (NY // BS, NX // BS), 0, 4) < 3).astype(jnp.int32), jax.random.fold_in(arg_keys[6], 1), 0, 1)
    return dict(mass=mass, tracer=tracer, uvel=uvel, vvel=vvel, case_east=case_east, case_north=case_north, ice_blocks=ice_blocks)


mass_floor = 0.1


def region(region_area, normal_pos, trans_pos, cell):
    values, grad_normal, grad_trans = cell
    centre_val = values + grad_normal * normal_pos + grad_trans * trans_pos
    carried = region_area * centre_val[0]
    return jnp.concatenate([carried[None], carried[None] * centre_val[1:]], axis=0)


def choose(forward, when_true, when_false):
    return tuple(jnp.where(forward, left_arr, right_arr) for left_arr, right_arr in zip(when_true, when_false))


def edge_flux(normal_speed, low_speed, high_speed, case_id, low_side, high_side, low_below, low_above, high_below, high_above):
    forward = normal_speed > 0.0
    signs = jnp.where(forward, 1.0, -1.0)
    reach = jnp.abs(normal_speed)
    source = choose(forward, low_side, high_side)
    beneath = choose(forward, low_below, high_below)
    overhead = choose(forward, low_above, high_above)
    summed = region(reach, signs * (0.5 - 0.5 * reach), 0.0, source)
    tri_normal = signs * (0.5 - reach / 3.0)
    low_area = jnp.where(case_id == 1, 0.5 * reach * low_speed, 0.0)
    low_offset = 0.5 - low_speed / 3.0
    summed = summed + region(low_area, tri_normal, low_offset, beneath) - region(low_area, tri_normal, -low_offset, source)
    high_area = jnp.where(case_id == 2, 0.5 * reach * high_speed, 0.0)
    high_offset = 0.5 - high_speed / 3.0
    summed = summed + region(high_area, tri_normal, -high_offset, overhead) - region(high_area, tri_normal, high_offset, source)
    return signs * summed


def category_fluxes(values, slopes, u_ext, v_ext, case_east_al, case_north_al, east_from, north_from):
    height = values.shape[1] - 2
    breadth = values.shape[2] - 2

    def along_x(row_sel, col_sel):
        return (values[:, row_sel, col_sel], slopes[0][:, row_sel, col_sel], slopes[1][:, row_sel, col_sel])

    def along_y(row_sel, col_sel):
        return (values[:, row_sel, col_sel], slopes[1][:, row_sel, col_sel], slopes[0][:, row_sel, col_sel])

    low_cols = slice(east_from + 1, breadth + 1)
    high_cols = slice(east_from + 2, breadth + 2)
    centre = slice(1, height + 1)
    below_rows = slice(0, height)
    above_rows = slice(2, height + 2)
    speed_east = 0.5 * (u_ext[centre, low_cols] + u_ext[below_rows, low_cols])
    east_flux = edge_flux(speed_east, jnp.abs(v_ext[below_rows, low_cols]), jnp.abs(v_ext[centre, low_cols]), case_east_al,
                          along_x(centre, low_cols), along_x(centre, high_cols), along_x(below_rows, low_cols),
                          along_x(above_rows, low_cols), along_x(below_rows, high_cols), along_x(above_rows, high_cols))
    low_rows = slice(north_from + 1, height + 1)
    high_rows = slice(north_from + 2, height + 2)
    centre_cols = slice(1, breadth + 1)
    west_cols = slice(0, breadth)
    east_cols = slice(2, breadth + 2)
    speed_north = 0.5 * (v_ext[low_rows, centre_cols] + v_ext[low_rows, west_cols])
    north_flux = edge_flux(speed_north, jnp.abs(u_ext[low_rows, west_cols]), jnp.abs(u_ext[low_rows, centre_cols]), case_north_al,
                           along_y(low_rows, centre_cols), along_y(high_rows, centre_cols), along_y(low_rows, west_cols),
                           along_y(low_rows, east_cols), along_y(high_rows, west_cols), along_y(high_rows, east_cols))
    return east_flux, north_flux


def all_fluxes(values, slopes, u_ext, v_ext, case_east_al, case_north_al, east_from, north_from):
    def per_category(paired):
        return category_fluxes(paired[0], paired[1], u_ext, v_ext, case_east_al, case_north_al, east_from, north_from)

    return lax.map(per_category, (values, slopes))


def slope_pair(extended):
    along_lon = 0.5 * (extended[..., 1:-1, 2:] - extended[..., 1:-1, :-2])
    along_lat = 0.5 * (extended[..., 2:, 1:-1] - extended[..., :-2, 1:-1])
    return jnp.stack([along_lon, along_lat], axis=1)


def update(fields, east_flux, north_flux):
    carried = fields[:, 0]
    conserved = jnp.concatenate([carried[:, None], carried[:, None] * fields[:, 1:]], axis=1)
    conserved = conserved - (east_flux[..., 1:] - east_flux[..., :-1]) - (north_flux[..., 1:, :] - north_flux[..., :-1, :])
    new_mass = conserved[:, 0]
    amounts = conserved[:, 1:] / jnp.maximum(new_mass, mass_floor)[:, None]
    return jnp.concatenate([new_mass[:, None], amounts], axis=1)


def extend(source_arr, margin):
    wrapped = jnp.concatenate([source_arr[..., -margin:], source_arr, source_arr[..., :margin]], axis=-1)
    folded = wrapped[..., ::-1, ::-1][..., :margin, :]
    bottom_rows = jnp.zeros(wrapped.shape[:-2] + (margin, wrapped.shape[-1]), jnp.float32)
    return jnp.concatenate([bottom_rows, wrapped, folded], axis=-2)


def reference(mass, tracer, uvel, vvel, case_east, case_north, ice_blocks):
    cell_mask = jnp.repeat(jnp.repeat(ice_blocks, BS, axis=0), BS, axis=1).astype(jnp.float32)
    fields = jnp.concatenate([(mass * cell_mask)[:, None], tracer], axis=1)
    u_ext = jnp.pad(jnp.concatenate([uvel[:, -1:], uvel, uvel[:, :1]], axis=1), ((1, 1), (0, 0)))
    v_ext = jnp.pad(jnp.concatenate([vvel[:, -1:], vvel, vvel[:, :1]], axis=1), ((1, 1), (0, 0)))
    case_east_al = jnp.concatenate([case_east[:, -1:], case_east], axis=1)
    case_north_al = jnp.concatenate([jnp.zeros((1, NX), jnp.int32), case_north], axis=0)
    for sweep in range(STEPS):
        extended = extend(fields, 2)
        slopes = slope_pair(extended)
        east_flux, north_flux = all_fluxes(extended[..., 1:-1, 1:-1], slopes, u_ext, v_ext, case_east_al, case_north_al, -1, -1)
        fields = update(fields, east_flux, north_flux)
    return fields[:, 0], fields[:, 1:]
```

```python
import functools

import jax
import jax.numpy as jnp
from jax import lax
from jax.experimental import pallas as pl
from jax.experimental.pallas import tpu as pltpu
from jax.sharding import PartitionSpec as P

STEPS = 2
NF = 8
FLOOR = 0.1
MESH = pl.DeviceIdType.MESH
BASE = 8
pick = jnp.where


def oriented(get, s, d):
    near = [pick(d, get(n, 1), get(n, -1)) for n in (-1, 0, 1, 2)]
    far = [pick(d, get(n, -1), get(n, 1)) for n in (0, 1)]
    two = [pick(d, get(n, 2), get(n, -2)) for n in (0, 1)]
    h = pick(s, get(0, 0), get(1, 0))
    b = pick(s, get(1, 0), get(0, 0))
    c = pick(s, get(-1, 0), get(2, 0))
    hd = pick(s, near[1], near[2])
    bd = pick(s, near[2], near[1])
    cd = pick(s, near[0], near[3])
    return h, b, c, hd, bd, cd, pick(s, far[0], far[1]), pick(s, two[0], two[1])


def mass_flux(get, geo):
    a, area, x1, x2, off, s, d = geo
    h, b, c, hd, bd, cd, hm, h2 = oriented(get, s, d)
    g = b - c
    w1 = a * (h + g * x1)
    w2 = area * (h + g * x2 + (hd - hm) * off)
    w3 = area * (hd + (bd - cd) * x2 - (h2 - h) * off)
    w2o = w2 * off
    w3o = w3 * off
    flux = w1 - w2 + w3
    ch = w1 - w2 + w3o
    cb = w1 * x1 - w2 * x2
    chd = w3 - w2o
    cbd = w3 * x2
    weights = (pick(s, ch, cb), pick(s, cb, ch), cb, pick(s, chd, cbd), pick(s, cbd, chd), cbd, w2o, w3o)
    return flux, weights


def tracer_flux(get, geo, weights):
    s, d = geo[5], geo[6]
    c0, c1, cb, e0, e1, cbd, chm, ch2 = weights
    total = c0 * get(0, 0) + c1 * get(1, 0) - cb * pick(s, get(-1, 0), get(2, 0))
    total += e0 * pick(d, get(0, 1), get(0, -1)) + e1 * pick(d, get(1, 1), get(1, -1))
    total -= cbd * pick(s, pick(d, get(-1, 1), get(-1, -1)), pick(d, get(2, 1), get(2, -1)))
    total += chm * pick(s, pick(d, get(0, -1), get(0, 1)), pick(d, get(1, -1), get(1, 1)))
    total -= ch2 * pick(s, pick(d, get(0, 2), get(0, -2)), pick(d, get(1, 2), get(1, -2)))
    return total


def edge_geometry(a, low, high, case):
    reach = jnp.abs(a)
    b = pick(case == 2.0, high, low)
    area = pick(case == 0.0, 0.0, 0.5 * a * b)
    return a, area, 0.25 - 0.25 * reach, 0.25 - reach / 6.0, 0.25 - b / 6.0, case


def remember(get):
    seen = {}

    def load(n, t):
        if (n, t) not in seen:
            seen[n, t] = get(n, t)
        return seen[n, t]

    return load


def kernel(nx, ny, ncat, height, breadth,
           mass_hbm, tracer_hbm, u_hbm, v_hbm, ce_hbm, cn_hbm, ice,
           mass_out, tracer_out,
           F, S, X, XM, FN, GF, CI, GE, GN, GS,
           ystage, yrecv, xsend, xrecv, gystage, gyrecv, gxsend, gxrecv,
           in_sem, out_sem, ys_sem, yr_sem, xs_sem, xr_sem, g_sem):
    gx = lax.axis_index("gx")
    gy = lax.axis_index("gy")
    bottom = gy == 0
    top = gy == ny - 1
    inner = gy > 0
    west = {"gx": lax.rem(gx + nx - 1, nx), "gy": gy}
    east = {"gx": lax.rem(gx + 1, nx), "gy": gy}
    south = {"gx": gx, "gy": jnp.maximum(gy - 1, 0)}
    north = {"gx": pick(top, nx - 1 - gx, gx), "gy": pick(top, gy, gy + 1)}
    north_slot = pick(top, 1, 0)
    tiles = height // 8
    rows = height + 2 * BASE
    inside = pl.ds(BASE, height)
    lane = lax.broadcasted_iota(jnp.int32, (8, breadth), 1)

    barrier = pltpu.get_barrier_semaphore()
    for where in (west, east, north):
        pl.semaphore_signal(barrier, inc=1, device_id=where, device_id_type=MESH)

    @pl.when(inner)
    def _():
        pl.semaphore_signal(barrier, inc=1, device_id=south, device_id_type=MESH)

    def load_mass(c):
        return pltpu.make_async_copy(mass_hbm.at[c], F.at[0, c, 0, inside], in_sem.at[0, c])

    def load_tracer(c):
        return pltpu.make_async_copy(tracer_hbm.at[c], F.at[0, c, pl.ds(1, NF - 1), inside], in_sem.at[1, c])

    geo_loads = [
        pltpu.make_async_copy(u_hbm, GF.at[0, inside], in_sem.at[2, 0]),
        pltpu.make_async_copy(v_hbm, GF.at[1, inside], in_sem.at[2, 1]),
        pltpu.make_async_copy(ce_hbm, CI.at[0], in_sem.at[2, 2]),
        pltpu.make_async_copy(cn_hbm, CI.at[1], in_sem.at[2, 3]),
    ]
    for copy in geo_loads:
        copy.start()
    for c in range(ncat):
        load_mass(c).start()
        load_tracer(c).start()

    def remote(src, dst, send, recv, to):
        return pltpu.make_async_remote_copy(src_ref=src, dst_ref=dst, send_sem=send, recv_sem=recv, device_id=to, device_id_type=MESH)

    def y_south(k, c):
        return remote(ystage.at[k, c, 0], yrecv.at[k, c, 1], ys_sem.at[k, c, 0], yr_sem.at[k, c, 1], south)

    def y_north(k, c):
        return remote(ystage.at[k, c, 1], yrecv.at[k, c, north_slot], ys_sem.at[k, c, 1], yr_sem.at[k, c, north_slot], north)

    def y_from(k, c, slot):
        return remote(ystage.at[k, c, slot], yrecv.at[k, c, slot], ys_sem.at[k, c, slot], yr_sem.at[k, c, slot], north)

    def x_west(k, c):
        return remote(xsend.at[k, c], xrecv.at[k, c, 1], xs_sem.at[k, c, 0], xr_sem.at[k, c, 1], west)

    def x_east(k, c):
        return remote(xsend.at[k, c], xrecv.at[k, c, 0], xs_sem.at[k, c, 1], xr_sem.at[k, c, 0], east)

    g_north = remote(gystage, gyrecv, g_sem.at[0], g_sem.at[1], north)
    g_east = remote(gxsend, gxrecv, g_sem.at[2], g_sem.at[3], east)

    def send_y(k, c):
        for f in range(NF):
            ystage[k, c, 0, pl.ds(2 * f, 2)] = F[k, c, f, pl.ds(BASE, 2)]
            ystage[k, c, 1, pl.ds(2 * f, 2)] = F[k, c, f, pl.ds(BASE + height - 2, 2)]

        @pl.when(top)
        def _():
            wide = (2 * NF, breadth)
            back = breadth - 1 - lax.broadcasted_iota(jnp.int32, wide, 1)
            row = lax.broadcasted_iota(jnp.int32, wide, 0)
            edge = jnp.take_along_axis(ystage[k, c, 1], back, axis=1)
            ystage[k, c, 1] = pick(lax.rem(row, 2) == 0, pltpu.roll(edge, 2 * NF - 1, 0), pltpu.roll(edge, 1, 0))

        @pl.when(inner)
        def _():
            y_south(k, c).start()

        y_north(k, c).start()

    def pack(source, target, fields):
        def tile(t, carry):
            packed = pltpu.roll(source(0)[pl.ds(BASE - 2 + 8 * t, 8)], 2, 1)
            for f in range(1, fields):
                moved = pltpu.roll(source(f)[pl.ds(BASE - 2 + 8 * t, 8)], 2 + 4 * f, 1)
                packed = pick(lane >= 4 * f, moved, packed)
            target[pl.ds(pl.multiple_of(8 * t, 8), 8)] = packed
            return carry

        lax.fori_loop(0, tiles + 1, tile, 0)

    def send_x(k, c):
        y_from(k, c, 1).wait_recv()
        for f in range(NF):
            F[k, c, f, pl.ds(BASE + height, 2)] = yrecv[k, c, 1, pl.ds(2 * f, 2)]

        @pl.when(inner)
        def _():
            y_from(k, c, 0).wait_recv()
            for f in range(NF):
                F[k, c, f, pl.ds(BASE - 2, 2)] = yrecv[k, c, 0, pl.ds(2 * f, 2)]

        @pl.when(bottom)
        def _():
            for f in range(NF):
                F[k, c, f, pl.ds(BASE - 2, 2)] = jnp.zeros((2, breadth), jnp.float32)

        pack(lambda f: F.at[k, c, f], xsend.at[k, c], NF)
        x_west(k, c).start()
        x_east(k, c).start()

    for copy in geo_loads:
        copy.wait()
    GF[2, inside] = CI[0].astype(jnp.float32)
    GF[3, inside] = CI[1].astype(jnp.float32)
    for f in range(4):
        gystage[pl.ds(f, 1)] = GF[f, pl.ds(BASE + height - 1, 1)]

    @pl.when(inner)
    def _():
        pl.semaphore_wait(barrier, 4)

    @pl.when(bottom)
    def _():
        pl.semaphore_wait(barrier, 3)

    @pl.when(jnp.logical_not(top))
    def _():
        g_north.start()

    block_rows = height // ice.shape[0]
    block_cols = breadth // ice.shape[1]

    def first(c, carry):
        load_mass(c).wait()
        load_tracer(c).wait()
        for r in range(ice.shape[0]):
            mask = jnp.zeros((block_rows, breadth), jnp.float32)
            wide = lax.broadcasted_iota(jnp.int32, (block_rows, breadth), 1)
            for q in range(ice.shape[1]):
                mask = pick(wide >= q * block_cols, ice[r, q].astype(jnp.float32), mask)
            band = pl.ds(BASE + r * block_rows, block_rows)
            F[0, c, 0, band] = F[0, c, 0, band] * mask
        send_y(0, c)
        return carry

    lax.fori_loop(0, ncat, first, 0)

    @pl.when(inner)
    def _():
        g_north.wait_recv()
        for f in range(4):
            GF[f, pl.ds(BASE - 1, 1)] = gyrecv[pl.ds(f, 1)]

    @pl.when(bottom)
    def _():
        for f in range(4):
            GF[f, pl.ds(BASE - 1, 1)] = jnp.zeros((1, breadth), jnp.float32)

    pack(lambda f: GF.at[f], gxsend, 4)
    g_east.start()

    def second(c, carry):
        send_x(0, c)
        return carry

    lax.fori_loop(0, ncat, second, 0)

    g_east.wait_recv()

    def save(where, at, values):
        for q, value in enumerate(values):
            where[q, at] = value

    def geometry(t, carry):
        here = pl.ds(pl.multiple_of(BASE + 8 * t, 8), 8)
        below = pl.ds(BASE - 1 + 8 * t, 8)
        at = pl.ds(pl.multiple_of(8 * t, 8), 8)
        u, v = GF[0, here], GF[1, here]
        u_below, v_below = GF[0, below], GF[1, below]
        save(GE, at, edge_geometry(0.5 * (u + u_below), jnp.abs(v_below), jnp.abs(v), GF[2, here]))
        mine, lower = gxrecv[pl.ds(2 + 8 * t, 8)], gxrecv[pl.ds(1 + 8 * t, 8)]

        def column(x, f):
            return jnp.broadcast_to(x[:, 4 * f + 1:4 * f + 2], (8, breadth))

        save(GS, at, edge_geometry(0.5 * (column(mine, 0) + column(lower, 0)), jnp.abs(column(lower, 1)), jnp.abs(column(mine, 1)), column(mine, 2)))
        return carry

    lax.fori_loop(0, tiles, geometry, 0)

    def north_geometry(t, carry):
        start = jnp.minimum(8 * t - 1, height - 8)
        here = pl.ds(BASE + start, 8)
        u, v, packed = GF[0, here], GF[1, here], gxrecv[pl.ds(2 + start, 8)]

        def from_west(x, f):
            return pltpu.roll(pick(lane == breadth - 1, pltpu.roll(packed, (breadth - 2 - 4 * f) % breadth, 1), x), 1, 1)

        u_west, v_west = from_west(u, 0), from_west(v, 1)
        save(GN, here, edge_geometry(0.5 * (v + v_west), jnp.abs(u_west), jnp.abs(u), GF[3, here]))
        return carry

    lax.fori_loop(0, tiles + 1, north_geometry, 0)

    def edges(where, at):
        a, area, x1, x2, off, case = (where[q, at] for q in range(6))
        return a, area, x1, x2, off, a > 0.0, case == 2.0

    def advance(k, c):
        def shift(t, carry):
            at = pl.ds(pl.multiple_of(8 * t, 8), 8)
            from_west, from_east, mine = xrecv[k, c, 0, at], xrecv[k, c, 1, at], xsend[k, c, at]
            left = lax.rem(lane, 4) < 2
            halo = pick(left, from_west, from_east)
            strip = pick(left, from_west, mine)
            X[at] = strip
            XM[at] = jnp.take_along_axis(strip, lax.rem(lane, 4), axis=1)
            for f in range(NF):
                value = F[k, c, f, pl.ds(BASE - 2 + 8 * t, 8)]
                side = pltpu.roll(halo, (breadth - 2 - 4 * f) % breadth, 1)
                S[0, f, at] = pltpu.roll(pick(lane >= breadth - 2, side, value), 2, 1)
                S[1, f, at] = pltpu.roll(pick(lane >= breadth - 1, side, value), 1, 1)
                S[2, f, at] = pltpu.roll(pick(lane < 1, side, value), breadth - 1, 1)
                S[3, f, at] = pltpu.roll(pick(lane < 2, side, value), breadth - 2, 1)
            return carry

        lax.fori_loop(0, tiles + 1, shift, 0)

        def reader(f, start):
            def get(row, col):
                if col == 0:
                    return F[k, c, f, pl.ds(BASE + start + row, 8)]
                return S[{-2: 0, -1: 1, 1: 2, 2: 3}[col], f, pl.ds(2 + start + row, 8)]

            return remember(get)

        def turned(get):
            return lambda n, t: get(t, n)

        def north_edges(start):
            at = pl.ds(BASE + start, 8)
            geo = edges(GN, at)
            flux, weights = mass_flux(reader(0, start), geo)
            found = [flux]
            for f in range(1, NF):
                found.append(tracer_flux(reader(f, start), geo, weights))
            for f in range(NF):
                FN[f, at] = found[f]
            return found

        north_edges(-1)

        def tile(t, carry):
            start = pl.multiple_of(8 * t, 8)
            at = pl.ds(start, 8)
            geo = edges(GS, at)

            def strip_reader(where):
                def get(row, col):
                    value = where[pl.ds(2 + start + row, 8)]
                    return value if col == 0 else pltpu.roll(value, (breadth - col) % breadth, 1)

                return remember(get)

            flux, weights = mass_flux(turned(strip_reader(XM)), geo)
            strip = pick(lane < 4, flux, tracer_flux(turned(strip_reader(X)), geo, weights))

            def divergence(f, east_flux):
                edge = pltpu.roll(strip, (breadth - 1 - 4 * f) % breadth, 1)
                return east_flux - pick(lane == 0, edge, pltpu.roll(east_flux, 1, 1))

            norths = north_edges(start)
            geo = edges(GE, at)
            flux, weights = mass_flux(turned(reader(0, start)), geo)
            after = pl.ds(BASE + start, 8)
            before = pl.ds(BASE - 1 + start, 8)
            mass = F[k, c, 0, after]
            new_mass = mass - divergence(0, flux) - (norths[0] - FN[0, before])
            F[k + 1, c, 0, after] = new_mass
            scale = 1.0 / jnp.maximum(new_mass, FLOOR)
            for f in range(1, NF):
                flux = tracer_flux(turned(reader(f, start)), geo, weights)
                amount = mass * F[k, c, f, after] - divergence(f, flux) - (norths[f] - FN[f, before])
                F[k + 1, c, f, after] = amount * scale
            return carry

        lax.fori_loop(0, tiles, tile, 0)

    def x_wait(k, c):
        x_east(k, c).wait_recv()
        x_west(k, c).wait_recv()

    def step_one(c, carry):
        x_wait(0, c)
        advance(0, c)
        send_y(1, c)

        @pl.when(c > 0)
        def _():
            send_x(1, c - 1)

        return carry

    lax.fori_loop(0, ncat, step_one, 0)
    send_x(1, ncat - 1)

    def save_mass(c):
        return pltpu.make_async_copy(F.at[2, c, 0, inside], mass_out.at[c], out_sem.at[0, c])

    def save_tracer(c):
        return pltpu.make_async_copy(F.at[2, c, pl.ds(1, NF - 1), inside], tracer_out.at[c], out_sem.at[1, c])

    def step_two(c, carry):
        x_wait(1, c)
        advance(1, c)
        save_mass(c).start()
        save_tracer(c).start()
        return carry

    lax.fori_loop(0, ncat, step_two, 0)

    @pl.when(jnp.logical_not(top))
    def _():
        g_north.wait_send()

    g_east.wait_send()

    def finish(c, carry):
        for k in range(STEPS):
            @pl.when(inner)
            def _():
                y_south(k, c).wait_send()

            y_north(k, c).wait_send()
            x_west(k, c).wait_send()
            x_east(k, c).wait_send()
        save_mass(c).wait()
        save_tracer(c).wait()
        return carry

    lax.fori_loop(0, ncat, finish, 0)


def solution(mesh):
    nx, ny = mesh.shape["gx"], mesh.shape["gy"]

    def per_device(mass, tracer, uvel, vvel, case_east, case_north, ice):
        ncat, height, breadth = mass.shape
        rows = height + 2 * BASE
        packed = height + 8
        f32 = jnp.float32
        hbm = pl.BlockSpec(memory_space=pl.ANY)
        return pl.pallas_call(
            functools.partial(kernel, nx, ny, ncat, height, breadth),
            out_shape=(jax.ShapeDtypeStruct(mass.shape, f32), jax.ShapeDtypeStruct(tracer.shape, f32)),
            in_specs=[hbm] * 6 + [pl.BlockSpec(memory_space=pltpu.SMEM)],
            out_specs=(hbm, hbm),
            scratch_shapes=[
                pltpu.VMEM((STEPS + 1, ncat, NF, rows, breadth), f32),
                pltpu.VMEM((4, NF, packed, breadth), f32),
                pltpu.VMEM((packed, breadth), f32),
                pltpu.VMEM((packed, breadth), f32),
                pltpu.VMEM((NF, packed, breadth), f32),
                pltpu.VMEM((4, rows, breadth), f32),
                pltpu.VMEM((2, height, breadth), jnp.int32),
                pltpu.VMEM((6, height, breadth), f32),
                pltpu.VMEM((6, packed, breadth), f32),
                pltpu.VMEM((6, height, breadth), f32),
                pltpu.VMEM((STEPS, ncat, 2, 2 * NF, breadth), f32),
                pltpu.VMEM((STEPS, ncat, 2, 2 * NF, breadth), f32),
                pltpu.VMEM((STEPS, ncat, packed, breadth), f32),
                pltpu.VMEM((STEPS, ncat, 2, packed, breadth), f32),
                pltpu.VMEM((8, breadth), f32),
                pltpu.VMEM((8, breadth), f32),
                pltpu.VMEM((packed, breadth), f32),
                pltpu.VMEM((packed, breadth), f32),
                pltpu.SemaphoreType.DMA((3, max(ncat, 4))),
                pltpu.SemaphoreType.DMA((2, ncat)),
                pltpu.SemaphoreType.DMA((STEPS, ncat, 2)),
                pltpu.SemaphoreType.DMA((STEPS, ncat, 2)),
                pltpu.SemaphoreType.DMA((STEPS, ncat, 2)),
                pltpu.SemaphoreType.DMA((STEPS, ncat, 2)),
                pltpu.SemaphoreType.DMA((4,)),
            ],
            compiler_params=pltpu.CompilerParams(collective_id=0, has_side_effects=True),
        )(mass, tracer, uvel, vvel, case_east, case_north, ice)

    placed = (P(None, "gy", "gx"), P(None, None, "gy", "gx")) + (P("gy", "gx"),) * 5
    return jax.shard_map(
        per_device,
        mesh=mesh,
        in_specs=placed,
        out_specs=(P(None, "gy", "gx"), P(None, None, "gy", "gx")),
        check_vma=False,
    )
```

```python
import functools

import jax
import jax.numpy as jnp
from jax import lax
from jax.experimental import pallas as pl
from jax.experimental.pallas import tpu as pltpu
from jax.sharding import PartitionSpec as P

STEPS = 2
NF = 8
FLOOR = 0.1
SHIFTS = (-2, -1, 1, 2)
MESH = pl.DeviceIdType.MESH
BASE = 8
pick = jnp.where


def oriented(get, s, d):
    near = [pick(d, get(n, 1), get(n, -1)) for n in (-1, 0, 1, 2)]
    far = [pick(d, get(n, -1), get(n, 1)) for n in (0, 1)]
    two = [pick(d, get(n, 2), get(n, -2)) for n in (0, 1)]
    h = pick(s, get(0, 0), get(1, 0))
    b = pick(s, get(1, 0), get(0, 0))
    c = pick(s, get(-1, 0), get(2, 0))
    hd = pick(s, near[1], near[2])
    bd = pick(s, near[2], near[1])
    cd = pick(s, near[0], near[3])
    return h, b, c, hd, bd, cd, pick(s, far[0], far[1]), pick(s, two[0], two[1])


def mass_flux(get, geo):
    a, area, x1, x2, off, s, d = geo
    h, b, c, hd, bd, cd, hm, h2 = oriented(get, s, d)
    g = b - c
    w1 = a * (h + g * x1)
    w2 = area * (h + g * x2 + (hd - hm) * off)
    w3 = area * (hd + (bd - cd) * x2 - (h2 - h) * off)
    w2o = w2 * off
    w3o = w3 * off
    flux = w1 - w2 + w3
    ch = w1 - w2 + w3o
    cb = w1 * x1 - w2 * x2
    chd = w3 - w2o
    cbd = w3 * x2
    zero = jnp.zeros_like(flux)
    points = {
        (0, 0): (pick(s, ch, cb), 1),
        (1, 0): (pick(s, cb, ch), 1),
        (-1, 0): (pick(s, cb, zero), -1),
        (2, 0): (pick(s, zero, cb), -1),
    }
    e0, e1 = pick(s, chd, cbd), pick(s, cbd, chd)
    back0, back1 = pick(s, w2o, zero), pick(s, zero, w2o)
    behind, beyond = pick(s, cbd, zero), pick(s, zero, cbd)
    far0, far1 = pick(s, w3o, zero), pick(s, zero, w3o)
    points[0, 1], points[0, -1] = (pick(d, e0, back0), 1), (pick(d, back0, e0), 1)
    points[1, 1], points[1, -1] = (pick(d, e1, back1), 1), (pick(d, back1, e1), 1)
    points[-1, 1], points[-1, -1] = (pick(d, behind, zero), -1), (pick(d, zero, behind), -1)
    points[2, 1], points[2, -1] = (pick(d, beyond, zero), -1), (pick(d, zero, beyond), -1)
    points[0, 2], points[0, -2] = (pick(d, far0, zero), -1), (pick(d, zero, far0), -1)
    points[1, 2], points[1, -2] = (pick(d, far1, zero), -1), (pick(d, zero, far1), -1)
    return flux, points


def edge_geometry(a, low, high, case):
    reach = jnp.abs(a)
    b = pick(case == 2.0, high, low)
    area = pick(case == 0.0, 0.0, 0.5 * a * b)
    return a, area, 0.25 - 0.25 * reach, 0.25 - reach / 6.0, 0.25 - b / 6.0, case


def remember(get):
    seen = {}

    def load(n, t):
        if (n, t) not in seen:
            seen[n, t] = get(n, t)
        return seen[n, t]

    return load


def kernel(nx, ny, ncat, height, breadth,
           mass_hbm, tracer_hbm, u_hbm, v_hbm, ce_hbm, cn_hbm, ice,
           mass_out, tracer_out,
           FA, FB, FC, SA, SB, ND, GF, CI, GE, GN, GW,
           ystage, yrecv, xsend, xrecv, gystage, gyrecv, gxsend, gxrecv,
           in_sem, out_sem, ys_sem, yr_sem, xs_sem, xr_sem, g_sem):
    F = (FA, FB, FC)
    gx = lax.axis_index("gx")
    gy = lax.axis_index("gy")
    bottom = gy == 0
    top = gy == ny - 1
    inner = gy > 0
    west = {"gx": lax.rem(gx + nx - 1, nx), "gy": gy}
    east = {"gx": lax.rem(gx + 1, nx), "gy": gy}
    south = {"gx": gx, "gy": jnp.maximum(gy - 1, 0)}
    north = {"gx": pick(top, nx - 1 - gx, gx), "gy": pick(top, gy, gy + 1)}
    north_slot = pick(top, 1, 0)
    tiles = height // 8
    rows = height + 2 * BASE
    inside = pl.ds(BASE, height)
    lane = lax.broadcasted_iota(jnp.int32, (8, breadth), 1)

    barrier = pltpu.get_barrier_semaphore()
    for where in (west, east, north):
        pl.semaphore_signal(barrier, inc=1, device_id=where, device_id_type=MESH)

    @pl.when(inner)
    def _():
        pl.semaphore_signal(barrier, inc=1, device_id=south, device_id_type=MESH)

    def load_mass(c):
        return pltpu.make_async_copy(mass_hbm.at[c], FA.at[c, 0, inside], in_sem.at[0, c])

    def load_tracer(c):
        return pltpu.make_async_copy(tracer_hbm.at[c], FA.at[c, pl.ds(1, NF - 1), inside], in_sem.at[1, c])

    geo_loads = [
        pltpu.make_async_copy(u_hbm, GF.at[0, inside], in_sem.at[2, 0]),
        pltpu.make_async_copy(v_hbm, GF.at[1, inside], in_sem.at[2, 1]),
        pltpu.make_async_copy(ce_hbm, CI.at[0], in_sem.at[2, 2]),
        pltpu.make_async_copy(cn_hbm, CI.at[1], in_sem.at[2, 3]),
    ]
    for copy in geo_loads:
        copy.start()
    for c in range(ncat):
        load_mass(c).start()
        load_tracer(c).start()

    def remote(src, dst, send, recv, to):
        return pltpu.make_async_remote_copy(src_ref=src, dst_ref=dst, send_sem=send, recv_sem=recv, device_id=to, device_id_type=MESH)

    def y_south(k, c):
        return remote(ystage.at[k, c, 0], yrecv.at[k, c, 1], ys_sem.at[k, c, 0], yr_sem.at[k, c, 1], south)

    def y_north(k, c):
        return remote(ystage.at[k, c, 1], yrecv.at[k, c, north_slot], ys_sem.at[k, c, 1], yr_sem.at[k, c, north_slot], north)

    def y_from(k, c, slot):
        return remote(ystage.at[k, c, slot], yrecv.at[k, c, slot], ys_sem.at[k, c, slot], yr_sem.at[k, c, slot], north)

    def x_west(k, c):
        return remote(xsend.at[k, c], xrecv.at[k, c, 1], xs_sem.at[k, c, 0], xr_sem.at[k, c, 1], west)

    def x_east(k, c):
        return remote(xsend.at[k, c], xrecv.at[k, c, 0], xs_sem.at[k, c, 1], xr_sem.at[k, c, 0], east)

    g_north = remote(gystage, gyrecv, g_sem.at[0], g_sem.at[1], north)
    g_east = remote(gxsend, gxrecv, g_sem.at[2], g_sem.at[3], east)

    def send_y(k, c):
        for f in range(NF):
            ystage[k, c, 0, pl.ds(2 * f, 2)] = F[k][c, f, pl.ds(BASE, 2)]
            ystage[k, c, 1, pl.ds(2 * f, 2)] = F[k][c, f, pl.ds(BASE + height - 2, 2)]

        @pl.when(top)
        def _():
            wide = (2 * NF, breadth)
            back = breadth - 1 - lax.broadcasted_iota(jnp.int32, wide, 1)
            row = lax.broadcasted_iota(jnp.int32, wide, 0)
            edge = jnp.take_along_axis(ystage[k, c, 1], back, axis=1)
            ystage[k, c, 1] = pick(lax.rem(row, 2) == 0, pltpu.roll(edge, 2 * NF - 1, 0), pltpu.roll(edge, 1, 0))

        @pl.when(inner)
        def _():
            y_south(k, c).start()

        y_north(k, c).start()

    def pack(source, target, fields):
        def tile(t, carry):
            packed = pltpu.roll(source(0)[pl.ds(BASE - 2 + 8 * t, 8)], 2, 1)
            for f in range(1, fields):
                moved = pltpu.roll(source(f)[pl.ds(BASE - 2 + 8 * t, 8)], 2 + 4 * f, 1)
                packed = pick(lane >= 4 * f, moved, packed)
            target[pl.ds(pl.multiple_of(8 * t, 8), 8)] = packed
            return carry

        lax.fori_loop(0, tiles + 1, tile, 0)

    def send_x(k, c):
        y_from(k, c, 1).wait_recv()
        for f in range(NF):
            F[k][c, f, pl.ds(BASE + height, 2)] = yrecv[k, c, 1, pl.ds(2 * f, 2)]

        @pl.when(inner)
        def _():
            y_from(k, c, 0).wait_recv()
            for f in range(NF):
                F[k][c, f, pl.ds(BASE - 2, 2)] = yrecv[k, c, 0, pl.ds(2 * f, 2)]

        @pl.when(bottom)
        def _():
            for f in range(NF):
                F[k][c, f, pl.ds(BASE - 2, 2)] = jnp.zeros((2, breadth), jnp.float32)

        pack(lambda f: F[k].at[c, f], xsend.at[k, c], NF)
        x_west(k, c).start()
        x_east(k, c).start()

    for copy in geo_loads:
        copy.wait()
    GF[2, inside] = CI[0].astype(jnp.float32)
    GF[3, inside] = CI[1].astype(jnp.float32)
    for f in range(4):
        gystage[pl.ds(f, 1)] = GF[f, pl.ds(BASE + height - 1, 1)]

    @pl.when(inner)
    def _():
        pl.semaphore_wait(barrier, 4)

    @pl.when(bottom)
    def _():
        pl.semaphore_wait(barrier, 3)

    @pl.when(jnp.logical_not(top))
    def _():
        g_north.start()

    block_rows = height // ice.shape[0]
    block_cols = breadth // ice.shape[1]

    def first(c, carry):
        load_mass(c).wait()
        load_tracer(c).wait()
        for r in range(ice.shape[0]):
            mask = jnp.zeros((block_rows, breadth), jnp.float32)
            wide = lax.broadcasted_iota(jnp.int32, (block_rows, breadth), 1)
            for q in range(ice.shape[1]):
                mask = pick(wide >= q * block_cols, ice[r, q].astype(jnp.float32), mask)
            band = pl.ds(BASE + r * block_rows, block_rows)
            FA[c, 0, band] = FA[c, 0, band] * mask
        send_y(0, c)
        return carry

    lax.fori_loop(0, ncat, first, 0)

    @pl.when(inner)
    def _():
        g_north.wait_recv()
        for f in range(4):
            GF[f, pl.ds(BASE - 1, 1)] = gyrecv[pl.ds(f, 1)]

    @pl.when(bottom)
    def _():
        for f in range(4):
            GF[f, pl.ds(BASE - 1, 1)] = jnp.zeros((1, breadth), jnp.float32)

    pack(lambda f: GF.at[f], gxsend, 4)
    g_east.start()

    def second(c, carry):
        send_x(0, c)
        return carry

    lax.fori_loop(0, ncat, second, 0)

    g_east.wait_recv()

    def save(where, at, values):
        for q, value in enumerate(values):
            where[q, at] = value

    def from_west(x, packed, f):
        return pltpu.roll(pick(lane == breadth - 1, pltpu.roll(packed, (breadth - 2 - 4 * f) % breadth, 1), x), 1, 1)

    def geometry(t, carry):
        here = pl.ds(pl.multiple_of(BASE + 8 * t, 8), 8)
        below = pl.ds(BASE - 1 + 8 * t, 8)
        at = pl.ds(pl.multiple_of(8 * t, 8), 8)
        u, v = GF[0, here], GF[1, here]
        u_below, v_below = GF[0, below], GF[1, below]
        save(GE, at, edge_geometry(0.5 * (u + u_below), jnp.abs(v_below), jnp.abs(v), GF[2, here]))
        mine, lower = gxrecv[pl.ds(2 + 8 * t, 8)], gxrecv[pl.ds(1 + 8 * t, 8)]
        u, u_below = from_west(u, mine, 0), from_west(u_below, lower, 0)
        v, v_below = from_west(v, mine, 1), from_west(v_below, lower, 1)
        save(GW, at, edge_geometry(0.5 * (u + u_below), jnp.abs(v_below), jnp.abs(v), from_west(GF[2, here], mine, 2)))
        return carry

    lax.fori_loop(0, tiles, geometry, 0)

    def north_geometry(t, carry):
        start = jnp.minimum(8 * t - 1, height - 8)
        here = pl.ds(BASE + start, 8)
        u, v, packed = GF[0, here], GF[1, here], gxrecv[pl.ds(2 + start, 8)]

        u_west, v_west = from_west(u, packed, 0), from_west(v, packed, 1)
        save(GN, here, edge_geometry(0.5 * (v + v_west), jnp.abs(u_west), jnp.abs(u), GF[3, here]))
        return carry

    lax.fori_loop(0, tiles + 1, north_geometry, 0)

    def edges(where, at):
        a, area, x1, x2, off, case = (where[q, at] for q in range(6))
        return a, area, x1, x2, off, a > 0.0, case == 2.0

    edge_lanes = (lane >= breadth - 2, lane >= breadth - 1, lane < 1, lane < 2)
    left = lax.rem(lane, 4) < 2

    def shift_tile(k, c, S, t):
        at = pl.ds(8 * t if isinstance(t, int) else pl.multiple_of(8 * t, 8), 8)
        halo = pick(left, xrecv[k, c, 0, at], xrecv[k, c, 1, at])

        def piece(f):
            value = F[k][c, f, pl.ds(BASE - 2 + 8 * t, 8)]
            side = pltpu.roll(halo, (breadth - 2 - 4 * f) % breadth, 1)
            for q, shift in enumerate(SHIFTS):
                S[q, f, at] = pltpu.roll(pick(edge_lanes[q], side, value), -shift % breadth, 1)

        return [functools.partial(piece, f) for f in range(NF)]

    def advance(k, c, S, ahead):
        def reader(f, start):
            def get(row, col):
                if col == 0:
                    return F[k][c, f, pl.ds(BASE + start + row, 8)]
                return S[SHIFTS.index(col), f, pl.ds(2 + start + row, 8)]

            return remember(get)

        def north_edges(get, start):
            at = pl.ds(BASE + start, 8)
            flux, points = mass_flux(get, edges(GN, at))
            ND[0, at] = flux
            for q, (value, _) in enumerate(points.values()):
                ND[1 + q, at] = value
            return flux, points

        north_edges(reader(0, -1), -1)
        for work in ahead(tiles):
            work()

        def tile(t, carry):
            start = pl.multiple_of(8 * t, 8)
            at = pl.ds(start, 8)
            after = pl.ds(BASE + start, 8)
            before = pl.ds(BASE - 1 + start, 8)
            work = ahead(t)
            get = reader(0, start)
            mass = get(0, 0)
            north, north_points = north_edges(get, start)
            if work:
                work[0]()
            east, east_points = mass_flux(lambda n, t: get(t, n), edges(GE, at))
            west, west_points = mass_flux(lambda n, t: get(t, n - 1), edges(GW, at))
            total = {(0, 0): mass}

            def add(where, value, sign):
                if where not in total:
                    total[where] = value if sign > 0 else -value
                elif sign > 0:
                    total[where] = total[where] + value
                else:
                    total[where] = total[where] - value

            for (n, q), (value, sign) in west_points.items():
                add((q, n - 1), value, sign)
            for i, ((n, q), (_, sign)) in enumerate(north_points.items()):
                add((n - 1, q), ND[1 + i, before], sign)
            for (n, q), (value, sign) in east_points.items():
                add((q, n), value, -sign)
            for (n, q), (value, sign) in north_points.items():
                add((n, q), value, -sign)
            new_mass = mass - (east - west) - (north - ND[0, before])
            F[k + 1][c, 0, after] = new_mass
            scale = 1.0 / jnp.maximum(new_mass, FLOOR)
            for f in range(1, NF):
                if work:
                    work[f]()
                get = reader(f, start)
                sums = [None, None]
                for i, ((row, col), value) in enumerate(total.items()):
                    term = value * get(row, col)
                    sums[i % 2] = term if sums[i % 2] is None else sums[i % 2] + term
                F[k + 1][c, f, after] = (sums[0] + sums[1]) * scale
            return carry

        lax.fori_loop(0, tiles, tile, 0)

    def x_wait(k, c):
        x_east(k, c).wait_recv()
        x_west(k, c).wait_recv()

    def save_mass(c):
        return pltpu.make_async_copy(FC.at[c, 0, inside], mass_out.at[c], out_sem.at[0, c])

    def save_tracer(c):
        return pltpu.make_async_copy(FC.at[c, pl.ds(1, NF - 1), inside], tracer_out.at[c], out_sem.at[1, c])

    order = [(k, c) for k in range(STEPS) for c in range(ncat)]
    x_wait(0, 0)

    def whole(t, carry):
        for work in shift_tile(0, 0, SA, t):
            work()
        return carry

    lax.fori_loop(0, tiles + 1, whole, 0)
    for i, (k, c) in enumerate(order):
        if i + 1 < len(order):
            x_wait(*order[i + 1])
            ahead = functools.partial(shift_tile, *order[i + 1], (SA, SB)[(i + 1) % 2])
        else:
            ahead = lambda t: []
        advance(k, c, (SA, SB)[i % 2], ahead)
        if k == 0:
            send_y(1, c)
        else:
            save_mass(c).start()
            save_tracer(c).start()
        if 1 <= i <= ncat:
            send_x(1, i - 1)

    @pl.when(jnp.logical_not(top))
    def _():
        g_north.wait_send()

    g_east.wait_send()

    def finish(c, carry):
        for k in range(STEPS):
            @pl.when(inner)
            def _():
                y_south(k, c).wait_send()

            y_north(k, c).wait_send()
            x_west(k, c).wait_send()
            x_east(k, c).wait_send()
        save_mass(c).wait()
        save_tracer(c).wait()
        return carry

    lax.fori_loop(0, ncat, finish, 0)


def solution(mesh):
    nx, ny = mesh.shape["gx"], mesh.shape["gy"]

    def per_device(mass, tracer, uvel, vvel, case_east, case_north, ice):
        ncat, height, breadth = mass.shape
        rows = height + 2 * BASE
        packed = height + 8
        f32 = jnp.float32
        hbm = pl.BlockSpec(memory_space=pl.ANY)
        return pl.pallas_call(
            functools.partial(kernel, nx, ny, ncat, height, breadth),
            out_shape=(jax.ShapeDtypeStruct(mass.shape, f32), jax.ShapeDtypeStruct(tracer.shape, f32)),
            in_specs=[hbm] * 6 + [pl.BlockSpec(memory_space=pltpu.SMEM)],
            out_specs=(hbm, hbm),
            scratch_shapes=[
                pltpu.VMEM((ncat, NF, rows, breadth), f32),
                pltpu.VMEM((ncat, NF, rows, breadth), f32),
                pltpu.VMEM((ncat, NF, rows, breadth), f32),
                pltpu.VMEM((4, NF, packed, breadth), f32),
                pltpu.VMEM((4, NF, packed, breadth), f32),
                pltpu.VMEM((17, packed, breadth), f32),
                pltpu.VMEM((4, rows, breadth), f32),
                pltpu.VMEM((2, height, breadth), jnp.int32),
                pltpu.VMEM((6, height, breadth), f32),
                pltpu.VMEM((6, packed, breadth), f32),
                pltpu.VMEM((6, height, breadth), f32),
                pltpu.VMEM((STEPS, ncat, 2, 2 * NF, breadth), f32),
                pltpu.VMEM((STEPS, ncat, 2, 2 * NF, breadth), f32),
                pltpu.VMEM((STEPS, ncat, packed, breadth), f32),
                pltpu.VMEM((STEPS, ncat, 2, packed, breadth), f32),
                pltpu.VMEM((8, breadth), f32),
                pltpu.VMEM((8, breadth), f32),
                pltpu.VMEM((packed, breadth), f32),
                pltpu.VMEM((packed, breadth), f32),
                pltpu.SemaphoreType.DMA((3, max(ncat, 4))),
                pltpu.SemaphoreType.DMA((2, ncat)),
                pltpu.SemaphoreType.DMA((STEPS, ncat, 2)),
                pltpu.SemaphoreType.DMA((STEPS, ncat, 2)),
                pltpu.SemaphoreType.DMA((STEPS, ncat, 2)),
                pltpu.SemaphoreType.DMA((STEPS, ncat, 2)),
                pltpu.SemaphoreType.DMA((4,)),
            ],
            compiler_params=pltpu.CompilerParams(collective_id=0, has_side_effects=True),
        )(mass, tracer, uvel, vvel, case_east, case_north, ice)

    placed = (P(None, "gy", "gx"), P(None, None, "gy", "gx")) + (P("gy", "gx"),) * 5
    return jax.shard_map(
        per_device,
        mesh=mesh,
        in_specs=placed,
        out_specs=(P(None, "gy", "gx"), P(None, None, "gy", "gx")),
        check_vma=False,
    )
```

```python
import functools

import jax
import jax.numpy as jnp
from jax import lax
from jax.experimental import pallas as pl
from jax.experimental.pallas import tpu as pltpu
from jax.sharding import PartitionSpec as P

STEPS = 2
NF = 8
FLOOR = 0.1
SHIFTS = (-2, -1, 1, 2)
MESH = pl.DeviceIdType.MESH
BASE = 8
pick = jnp.where


def oriented(get, s, d):
    near = [pick(d, get(n, 1), get(n, -1)) for n in (-1, 0, 1, 2)]
    far = [pick(d, get(n, -1), get(n, 1)) for n in (0, 1)]
    two = [pick(d, get(n, 2), get(n, -2)) for n in (0, 1)]
    h = pick(s, get(0, 0), get(1, 0))
    b = pick(s, get(1, 0), get(0, 0))
    c = pick(s, get(-1, 0), get(2, 0))
    hd = pick(s, near[1], near[2])
    bd = pick(s, near[2], near[1])
    cd = pick(s, near[0], near[3])
    return h, b, c, hd, bd, cd, pick(s, far[0], far[1]), pick(s, two[0], two[1])


def mass_flux(get, geo):
    a, area, x1, x2, off, s, d = geo
    h, b, c, hd, bd, cd, hm, h2 = oriented(get, s, d)
    g = b - c
    w1 = a * (h + g * x1)
    w2 = area * (h + g * x2 + (hd - hm) * off)
    w3 = area * (hd + (bd - cd) * x2 - (h2 - h) * off)
    w2o = w2 * off
    w3o = w3 * off
    flux = w1 - w2 + w3
    ch = w1 - w2 + w3o
    cb = w1 * x1 - w2 * x2
    chd = w3 - w2o
    cbd = w3 * x2
    zero = jnp.zeros_like(flux)
    points = {
        (0, 0): (pick(s, ch, cb), 1),
        (1, 0): (pick(s, cb, ch), 1),
        (-1, 0): (pick(s, cb, zero), -1),
        (2, 0): (pick(s, zero, cb), -1),
    }
    e0, e1 = pick(s, chd, cbd), pick(s, cbd, chd)
    back0, back1 = pick(s, w2o, zero), pick(s, zero, w2o)
    behind, beyond = pick(s, cbd, zero), pick(s, zero, cbd)
    far0, far1 = pick(s, w3o, zero), pick(s, zero, w3o)
    points[0, 1], points[0, -1] = (pick(d, e0, back0), 1), (pick(d, back0, e0), 1)
    points[1, 1], points[1, -1] = (pick(d, e1, back1), 1), (pick(d, back1, e1), 1)
    points[-1, 1], points[-1, -1] = (pick(d, behind, zero), -1), (pick(d, zero, behind), -1)
    points[2, 1], points[2, -1] = (pick(d, beyond, zero), -1), (pick(d, zero, beyond), -1)
    points[0, 2], points[0, -2] = (pick(d, far0, zero), -1), (pick(d, zero, far0), -1)
    points[1, 2], points[1, -2] = (pick(d, far1, zero), -1), (pick(d, zero, far1), -1)
    return flux, points


def edge_geometry(a, low, high, case):
    reach = jnp.abs(a)
    b = pick(case == 2.0, high, low)
    area = pick(case == 0.0, 0.0, 0.5 * a * b)
    return a, area, 0.25 - 0.25 * reach, 0.25 - reach / 6.0, 0.25 - b / 6.0, case


def remember(get):
    seen = {}

    def load(n, t):
        if (n, t) not in seen:
            seen[n, t] = get(n, t)
        return seen[n, t]

    return load


def kernel(nx, ny, ncat, height, breadth,
           mass_hbm, tracer_hbm, u_hbm, v_hbm, ce_hbm, cn_hbm, ice,
           mass_out, tracer_out,
           FA, FB, SA, SB, ND, GF, CI, GE, GN, GW,
           ystage, yrecv, xsend, xrecv, gystage, gyrecv, gxsend, gxrecv,
           in_sem, ys_sem, yr_sem, xs_sem, xr_sem, g_sem):
    F = (FA, FB)
    gx = lax.axis_index("gx")
    gy = lax.axis_index("gy")
    bottom = gy == 0
    top = gy == ny - 1
    inner = gy > 0
    west = {"gx": lax.rem(gx + nx - 1, nx), "gy": gy}
    east = {"gx": lax.rem(gx + 1, nx), "gy": gy}
    south = {"gx": gx, "gy": jnp.maximum(gy - 1, 0)}
    north = {"gx": pick(top, nx - 1 - gx, gx), "gy": pick(top, gy, gy + 1)}
    north_slot = pick(top, 1, 0)
    tiles = height // 8
    rows = height + 2 * BASE
    inside = pl.ds(BASE, height)
    lane = lax.broadcasted_iota(jnp.int32, (8, breadth), 1)

    barrier = pltpu.get_barrier_semaphore()
    for where in (west, east, north):
        pl.semaphore_signal(barrier, inc=1, device_id=where, device_id_type=MESH)

    @pl.when(inner)
    def _():
        pl.semaphore_signal(barrier, inc=1, device_id=south, device_id_type=MESH)

    def load_mass(c):
        return pltpu.make_async_copy(mass_hbm.at[c], FA.at[c, 0, inside], in_sem.at[0, c])

    def load_tracer(c):
        return pltpu.make_async_copy(tracer_hbm.at[c], FA.at[c, pl.ds(1, NF - 1), inside], in_sem.at[1, c])

    geo_loads = [
        pltpu.make_async_copy(u_hbm, GF.at[0, inside], in_sem.at[2, 0]),
        pltpu.make_async_copy(v_hbm, GF.at[1, inside], in_sem.at[2, 1]),
        pltpu.make_async_copy(ce_hbm, CI.at[0], in_sem.at[2, 2]),
        pltpu.make_async_copy(cn_hbm, CI.at[1], in_sem.at[2, 3]),
    ]
    for copy in geo_loads:
        copy.start()
    for c in range(ncat):
        load_mass(c).start()
        load_tracer(c).start()

    def remote(src, dst, send, recv, to):
        return pltpu.make_async_remote_copy(src_ref=src, dst_ref=dst, send_sem=send, recv_sem=recv, device_id=to, device_id_type=MESH)

    def y_south(k, c):
        return remote(ystage.at[k, c, 0], yrecv.at[k, c, 1], ys_sem.at[k, c, 0], yr_sem.at[k, c, 1], south)

    def y_north(k, c):
        return remote(ystage.at[k, c, 1], yrecv.at[k, c, north_slot], ys_sem.at[k, c, 1], yr_sem.at[k, c, north_slot], north)

    def y_from(k, c, slot):
        return remote(ystage.at[k, c, slot], yrecv.at[k, c, slot], ys_sem.at[k, c, slot], yr_sem.at[k, c, slot], north)

    def x_west(k, c):
        return remote(xsend.at[k, c], xrecv.at[k, c, 1], xs_sem.at[k, c, 0], xr_sem.at[k, c, 1], west)

    def x_east(k, c):
        return remote(xsend.at[k, c], xrecv.at[k, c, 0], xs_sem.at[k, c, 1], xr_sem.at[k, c, 0], east)

    g_north = remote(gystage, gyrecv, g_sem.at[0], g_sem.at[1], north)
    g_east = remote(gxsend, gxrecv, g_sem.at[2], g_sem.at[3], east)

    def send_y(k, c):
        for f in range(NF):
            ystage[k, c, 0, pl.ds(2 * f, 2)] = F[k][c, f, pl.ds(BASE, 2)]
            ystage[k, c, 1, pl.ds(2 * f, 2)] = F[k][c, f, pl.ds(BASE + height - 2, 2)]

        @pl.when(top)
        def _():
            wide = (2 * NF, breadth)
            back = breadth - 1 - lax.broadcasted_iota(jnp.int32, wide, 1)
            row = lax.broadcasted_iota(jnp.int32, wide, 0)
            edge = jnp.take_along_axis(ystage[k, c, 1], back, axis=1)
            ystage[k, c, 1] = pick(lax.rem(row, 2) == 0, pltpu.roll(edge, 2 * NF - 1, 0), pltpu.roll(edge, 1, 0))

        @pl.when(inner)
        def _():
            y_south(k, c).start()

        y_north(k, c).start()

    def packed(values):
        found = pltpu.roll(values[0], 2, 1)
        for f in range(1, len(values)):
            found = pick(lane >= 4 * f, pltpu.roll(values[f], 2 + 4 * f, 1), found)
        return found

    def pack(source, target, fields, first, count):
        def tile(t, carry):
            at = first + 8 * t
            target[pl.ds(2 + at, 8)] = packed([source(f)[pl.ds(BASE + at, 8)] for f in range(fields)])
            return carry

        lax.fori_loop(0, count, tile, 0, unroll=4 if count % 4 == 0 else 3)

    def pack_rim(k, c):
        for at in (-2, height - 6):
            xsend[k, c, pl.ds(2 + at, 8)] = packed([F[k][c, f, pl.ds(BASE + at, 8)] for f in range(NF)])

    def send_x(k, c):
        y_from(k, c, 1).wait_recv()
        for f in range(NF):
            F[k][c, f, pl.ds(BASE + height, 2)] = yrecv[k, c, 1, pl.ds(2 * f, 2)]

        @pl.when(inner)
        def _():
            y_from(k, c, 0).wait_recv()
            for f in range(NF):
                F[k][c, f, pl.ds(BASE - 2, 2)] = yrecv[k, c, 0, pl.ds(2 * f, 2)]

        @pl.when(bottom)
        def _():
            for f in range(NF):
                F[k][c, f, pl.ds(BASE - 2, 2)] = jnp.zeros((2, breadth), jnp.float32)

        pack_rim(k, c)
        x_west(k, c).start()
        x_east(k, c).start()

    for copy in geo_loads:
        copy.wait()
    GF[2, inside] = CI[0].astype(jnp.float32)
    GF[3, inside] = CI[1].astype(jnp.float32)
    for f in range(4):
        gystage[pl.ds(f, 1)] = GF[f, pl.ds(BASE + height - 1, 1)]

    @pl.when(inner)
    def _():
        pl.semaphore_wait(barrier, 4)

    @pl.when(bottom)
    def _():
        pl.semaphore_wait(barrier, 3)

    @pl.when(jnp.logical_not(top))
    def _():
        g_north.start()

    block_rows = height // ice.shape[0]
    block_cols = breadth // ice.shape[1]

    def first(c, carry):
        load_mass(c).wait()
        load_tracer(c).wait()
        for r in range(ice.shape[0]):
            mask = jnp.zeros((block_rows, breadth), jnp.float32)
            wide = lax.broadcasted_iota(jnp.int32, (block_rows, breadth), 1)
            for q in range(ice.shape[1]):
                mask = pick(wide >= q * block_cols, ice[r, q].astype(jnp.float32), mask)
            band = pl.ds(BASE + r * block_rows, block_rows)
            FA[c, 0, band] = FA[c, 0, band] * mask
        send_y(0, c)
        return carry

    lax.fori_loop(0, ncat, first, 0)

    def columns(c, carry):
        pack(lambda f: FA.at[c, f], xsend.at[0, c], NF, 0, tiles)
        return carry

    lax.fori_loop(0, ncat, columns, 0)

    @pl.when(inner)
    def _():
        g_north.wait_recv()
        for f in range(4):
            GF[f, pl.ds(BASE - 1, 1)] = gyrecv[pl.ds(f, 1)]

    @pl.when(bottom)
    def _():
        for f in range(4):
            GF[f, pl.ds(BASE - 1, 1)] = jnp.zeros((1, breadth), jnp.float32)

    pack(lambda f: GF.at[f], gxsend, 4, -2, tiles + 1)
    g_east.start()

    def second(c, carry):
        send_x(0, c)
        return carry

    lax.fori_loop(0, ncat, second, 0)


    def save(where, at, values):
        for q, value in enumerate(values):
            where[q, at] = value

    def from_west(x, packed, f):
        return pltpu.roll(pick(lane == breadth - 1, pltpu.roll(packed, (breadth - 2 - 4 * f) % breadth, 1), x), 1, 1)

    def geometry(t, carry):
        here = pl.ds(pl.multiple_of(BASE + 8 * t, 8), 8)
        below = pl.ds(BASE - 1 + 8 * t, 8)
        at = pl.ds(pl.multiple_of(8 * t, 8), 8)
        u, v = GF[0, here], GF[1, here]
        u_below, v_below = GF[0, below], GF[1, below]
        save(GE, at, edge_geometry(0.5 * (u + u_below), jnp.abs(v_below), jnp.abs(v), GF[2, here]))
        return carry

    lax.fori_loop(0, tiles, geometry, 0, unroll=2)
    g_east.wait_recv()

    def west_geometry(t, carry):
        here = pl.ds(pl.multiple_of(BASE + 8 * t, 8), 8)
        below = pl.ds(BASE - 1 + 8 * t, 8)
        at = pl.ds(pl.multiple_of(8 * t, 8), 8)
        u, v = GF[0, here], GF[1, here]
        u_below, v_below = GF[0, below], GF[1, below]
        mine, lower = gxrecv[pl.ds(2 + 8 * t, 8)], gxrecv[pl.ds(1 + 8 * t, 8)]
        u, u_below = from_west(u, mine, 0), from_west(u_below, lower, 0)
        v, v_below = from_west(v, mine, 1), from_west(v_below, lower, 1)
        save(GW, at, edge_geometry(0.5 * (u + u_below), jnp.abs(v_below), jnp.abs(v), from_west(GF[2, here], mine, 2)))
        return carry

    lax.fori_loop(0, tiles, west_geometry, 0, unroll=2)

    def north_geometry(t, carry):
        start = jnp.minimum(8 * t - 1, height - 8)
        here = pl.ds(BASE + start, 8)
        u, v, packed = GF[0, here], GF[1, here], gxrecv[pl.ds(2 + start, 8)]

        u_west, v_west = from_west(u, packed, 0), from_west(v, packed, 1)
        save(GN, here, edge_geometry(0.5 * (v + v_west), jnp.abs(u_west), jnp.abs(u), GF[3, here]))
        return carry

    lax.fori_loop(0, tiles + 1, north_geometry, 0, unroll=3)

    def edges(where, at):
        a, area, x1, x2, off, case = (where[q, at] for q in range(6))
        return a, area, x1, x2, off, a > 0.0, case == 2.0

    edge_lanes = (lane >= breadth - 2, lane >= breadth - 1, lane < 1, lane < 2)
    left = lax.rem(lane, 4) < 2

    def shift_tile(k, c, S, t):
        at = pl.ds(8 * t if isinstance(t, int) else pl.multiple_of(8 * t, 8), 8)
        halo = pick(left, xrecv[k, c, 0, at], xrecv[k, c, 1, at])

        def piece(f):
            value = F[k][c, f, pl.ds(BASE - 2 + 8 * t, 8)]
            side = pltpu.roll(halo, (breadth - 2 - 4 * f) % breadth, 1)
            for q, shift in enumerate(SHIFTS):
                S[q, f, at] = pltpu.roll(pick(edge_lanes[q], side, value), -shift % breadth, 1)

        return [functools.partial(piece, f) for f in range(NF)]

    def advance(k, c, S, ahead):
        def reader(f, start):
            def get(row, col):
                if col == 0:
                    return F[k][c, f, pl.ds(BASE + start + row, 8)]
                return S[SHIFTS.index(col), f, pl.ds(2 + start + row, 8)]

            return remember(get)

        def north_edges(get, start):
            at = pl.ds(BASE + start, 8)
            flux, points = mass_flux(get, edges(GN, at))
            ND[0, at] = flux
            for q, (value, _) in enumerate(points.values()):
                ND[1 + q, at] = value
            return flux, points

        north_edges(reader(0, -1), -1)
        for work in ahead(tiles):
            work()

        def tile(t, carry):
            start = pl.multiple_of(8 * t, 8)
            at = pl.ds(start, 8)
            after = pl.ds(BASE + start, 8)
            before = pl.ds(BASE - 1 + start, 8)
            work = ahead(t)
            get = reader(0, start)
            mass = get(0, 0)
            north, north_points = north_edges(get, start)
            if work:
                work[0]()
            east, east_points = mass_flux(lambda n, t: get(t, n), edges(GE, at))
            west, west_points = mass_flux(lambda n, t: get(t, n - 1), edges(GW, at))
            total = {(0, 0): mass}

            def emit(f, value):
                if k + 1 < STEPS:
                    F[k + 1][c, f, after] = value
                elif f:
                    tracer_out[c, f - 1, at] = value
                else:
                    mass_out[c, at] = value


            def add(where, value, sign):
                if where not in total:
                    total[where] = value if sign > 0 else -value
                elif sign > 0:
                    total[where] = total[where] + value
                else:
                    total[where] = total[where] - value

            for (n, q), (value, sign) in west_points.items():
                add((q, n - 1), value, sign)
            for i, ((n, q), (_, sign)) in enumerate(north_points.items()):
                add((n - 1, q), ND[1 + i, before], sign)
            for (n, q), (value, sign) in east_points.items():
                add((q, n), value, -sign)
            for (n, q), (value, sign) in north_points.items():
                add((n, q), value, -sign)
            new_mass = mass - (east - west) - (north - ND[0, before])
            emit(0, new_mass)
            scale = 1.0 / jnp.maximum(new_mass, FLOOR)
            for f in range(1, NF):
                if work:
                    work[f]()
                get = reader(f, start)
                sums = [None, None]
                for i, ((row, col), value) in enumerate(total.items()):
                    term = value * get(row, col)
                    sums[i % 2] = term if sums[i % 2] is None else sums[i % 2] + term
                emit(f, (sums[0] + sums[1]) * scale)
            return carry

        lax.fori_loop(0, tiles, tile, 0)
        if k + 1 < STEPS:
            pack(lambda f: F[k + 1].at[c, f], xsend.at[k + 1, c], NF, 0, tiles)

    def x_wait(k, c):
        x_east(k, c).wait_recv()
        x_west(k, c).wait_recv()

    order = [(k, c) for k in range(STEPS) for c in range(ncat)]
    x_wait(0, 0)

    def whole(t, carry):
        for work in shift_tile(0, 0, SA, t):
            work()
        return carry

    lax.fori_loop(0, tiles + 1, whole, 0, unroll=3)
    for i, (k, c) in enumerate(order):
        if i + 1 < len(order):
            x_wait(*order[i + 1])
            ahead = functools.partial(shift_tile, *order[i + 1], (SA, SB)[(i + 1) % 2])
        else:
            ahead = lambda t: []
        advance(k, c, (SA, SB)[i % 2], ahead)
        if k == 0:
            send_y(1, c)
        if 1 <= i <= ncat:
            send_x(1, i - 1)

    @pl.when(jnp.logical_not(top))
    def _():
        g_north.wait_send()

    g_east.wait_send()

    def finish(c, carry):
        for k in range(STEPS):
            @pl.when(inner)
            def _():
                y_south(k, c).wait_send()

            y_north(k, c).wait_send()
            x_west(k, c).wait_send()
            x_east(k, c).wait_send()
        return carry

    lax.fori_loop(0, ncat, finish, 0)


def solution(mesh):
    nx, ny = mesh.shape["gx"], mesh.shape["gy"]

    def per_device(mass, tracer, uvel, vvel, case_east, case_north, ice):
        ncat, height, breadth = mass.shape
        rows = height + 2 * BASE
        packed = height + 8
        f32 = jnp.float32
        hbm = pl.BlockSpec(memory_space=pl.ANY)
        return pl.pallas_call(
            functools.partial(kernel, nx, ny, ncat, height, breadth),
            out_shape=(pltpu.VMEM(mass.shape, f32), pltpu.VMEM(tracer.shape, f32)),
            in_specs=[hbm] * 6 + [pl.BlockSpec(memory_space=pltpu.SMEM)],
            out_specs=(pl.BlockSpec(memory_space=pltpu.VMEM),) * 2,
            scratch_shapes=[
                pltpu.VMEM((ncat, NF, rows, breadth), f32),
                pltpu.VMEM((ncat, NF, rows, breadth), f32),
                pltpu.VMEM((4, NF, packed, breadth), f32),
                pltpu.VMEM((4, NF, packed, breadth), f32),
                pltpu.VMEM((17, packed, breadth), f32),
                pltpu.VMEM((4, rows, breadth), f32),
                pltpu.VMEM((2, height, breadth), jnp.int32),
                pltpu.VMEM((6, height, breadth), f32),
                pltpu.VMEM((6, packed, breadth), f32),
                pltpu.VMEM((6, height, breadth), f32),
                pltpu.VMEM((STEPS, ncat, 2, 2 * NF, breadth), f32),
                pltpu.VMEM((STEPS, ncat, 2, 2 * NF, breadth), f32),
                pltpu.VMEM((STEPS, ncat, packed, breadth), f32),
                pltpu.VMEM((STEPS, ncat, 2, packed, breadth), f32),
                pltpu.VMEM((8, breadth), f32),
                pltpu.VMEM((8, breadth), f32),
                pltpu.VMEM((packed, breadth), f32),
                pltpu.VMEM((packed, breadth), f32),
                pltpu.SemaphoreType.DMA((3, max(ncat, 4))),
                pltpu.SemaphoreType.DMA((STEPS, ncat, 2)),
                pltpu.SemaphoreType.DMA((STEPS, ncat, 2)),
                pltpu.SemaphoreType.DMA((STEPS, ncat, 2)),
                pltpu.SemaphoreType.DMA((STEPS, ncat, 2)),
                pltpu.SemaphoreType.DMA((4,)),
            ],
            compiler_params=pltpu.CompilerParams(collective_id=0, has_side_effects=True),
        )(mass, tracer, uvel, vvel, case_east, case_north, ice)

    placed = (P(None, "gy", "gx"), P(None, None, "gy", "gx")) + (P("gy", "gx"),) * 5
    return jax.shard_map(
        per_device,
        mesh=mesh,
        in_specs=placed,
        out_specs=(P(None, "gy", "gx"), P(None, None, "gy", "gx")),
        check_vma=False,
    )
```

```python
import functools

import jax
import jax.numpy as jnp
from jax import lax
from jax.experimental import pallas as pl
from jax.experimental.pallas import tpu as pltpu
from jax.sharding import PartitionSpec as P

STEPS = 2
NF = 8
FLOOR = 0.1
SHIFTS = (-2, -1, 1, 2)
MESH = pl.DeviceIdType.MESH
BASE = 8
pick = jnp.where


def oriented(get, s, d):
    near = [pick(d, get(n, 1), get(n, -1)) for n in (-1, 0, 1, 2)]
    far = [pick(d, get(n, -1), get(n, 1)) for n in (0, 1)]
    two = [pick(d, get(n, 2), get(n, -2)) for n in (0, 1)]
    h = pick(s, get(0, 0), get(1, 0))
    b = pick(s, get(1, 0), get(0, 0))
    c = pick(s, get(-1, 0), get(2, 0))
    hd = pick(s, near[1], near[2])
    bd = pick(s, near[2], near[1])
    cd = pick(s, near[0], near[3])
    return h, b, c, hd, bd, cd, pick(s, far[0], far[1]), pick(s, two[0], two[1])


def mass_flux(get, geo):
    a, area, x1, x2, off, s, d = geo
    h, b, c, hd, bd, cd, hm, h2 = oriented(get, s, d)
    g = b - c
    w1 = a * (h + g * x1)
    w2 = area * (h + g * x2 + (hd - hm) * off)
    w3 = area * (hd + (bd - cd) * x2 - (h2 - h) * off)
    w2o = w2 * off
    w3o = w3 * off
    flux = w1 - w2 + w3
    ch = w1 - w2 + w3o
    cb = w1 * x1 - w2 * x2
    chd = w3 - w2o
    cbd = w3 * x2
    zero = jnp.zeros_like(flux)
    points = {
        (0, 0): (pick(s, ch, cb), 1),
        (1, 0): (pick(s, cb, ch), 1),
        (-1, 0): (pick(s, cb, zero), -1),
        (2, 0): (pick(s, zero, cb), -1),
    }
    e0, e1 = pick(s, chd, cbd), pick(s, cbd, chd)
    back0, back1 = pick(s, w2o, zero), pick(s, zero, w2o)
    behind, beyond = pick(s, cbd, zero), pick(s, zero, cbd)
    far0, far1 = pick(s, w3o, zero), pick(s, zero, w3o)
    points[0, 1], points[0, -1] = (pick(d, e0, back0), 1), (pick(d, back0, e0), 1)
    points[1, 1], points[1, -1] = (pick(d, e1, back1), 1), (pick(d, back1, e1), 1)
    points[-1, 1], points[-1, -1] = (pick(d, behind, zero), -1), (pick(d, zero, behind), -1)
    points[2, 1], points[2, -1] = (pick(d, beyond, zero), -1), (pick(d, zero, beyond), -1)
    points[0, 2], points[0, -2] = (pick(d, far0, zero), -1), (pick(d, zero, far0), -1)
    points[1, 2], points[1, -2] = (pick(d, far1, zero), -1), (pick(d, zero, far1), -1)
    return flux, points


def edge_geometry(a, low, high, case):
    reach = jnp.abs(a)
    b = pick(case == 2.0, high, low)
    area = pick(case == 0.0, 0.0, 0.5 * a * b)
    return a, area, 0.25 - 0.25 * reach, 0.25 - reach / 6.0, 0.25 - b / 6.0, case


def remember(get):
    seen = {}

    def load(n, t):
        if (n, t) not in seen:
            seen[n, t] = get(n, t)
        return seen[n, t]

    return load


def kernel(nx, ny, ncat, height, breadth,
           mass_hbm, tracer_hbm, u_hbm, v_hbm, ce_hbm, cn_hbm, ice,
           mass_out, tracer_out,
           FA, FB, SA, SB, ND, GF, CI, GE, GN, GW,
           ystage, yrecv, xsend, xrecv, gystage, gyrecv, gxsend, gxrecv,
           in_sem, ys_sem, yr_sem, xs_sem, xr_sem, g_sem):
    F = (FA, FB)
    gx = lax.axis_index("gx")
    gy = lax.axis_index("gy")
    bottom = gy == 0
    top = gy == ny - 1
    inner = gy > 0
    west = {"gx": lax.rem(gx + nx - 1, nx), "gy": gy}
    east = {"gx": lax.rem(gx + 1, nx), "gy": gy}
    south = {"gx": gx, "gy": jnp.maximum(gy - 1, 0)}
    north = {"gx": pick(top, nx - 1 - gx, gx), "gy": pick(top, gy, gy + 1)}
    north_slot = pick(top, 1, 0)
    tiles = height // 8
    rows = height + 2 * BASE
    inside = pl.ds(BASE, height)
    lane = lax.broadcasted_iota(jnp.int32, (8, breadth), 1)

    barrier = pltpu.get_barrier_semaphore()
    for where in (west, east, north):
        pl.semaphore_signal(barrier, inc=1, device_id=where, device_id_type=MESH)

    @pl.when(inner)
    def _():
        pl.semaphore_signal(barrier, inc=1, device_id=south, device_id_type=MESH)

    def load_mass(c):
        return pltpu.make_async_copy(mass_hbm.at[c], FA.at[c, 0, inside], in_sem.at[0, c])

    def load_tracer(c):
        return pltpu.make_async_copy(tracer_hbm.at[c], FA.at[c, pl.ds(1, NF - 1), inside], in_sem.at[1, c])

    geo_loads = [
        pltpu.make_async_copy(u_hbm, GF.at[0, inside], in_sem.at[2, 0]),
        pltpu.make_async_copy(v_hbm, GF.at[1, inside], in_sem.at[2, 1]),
        pltpu.make_async_copy(ce_hbm, CI.at[0], in_sem.at[2, 2]),
        pltpu.make_async_copy(cn_hbm, CI.at[1], in_sem.at[2, 3]),
    ]
    for copy in geo_loads:
        copy.start()
    for c in range(ncat):
        load_mass(c).start()
        load_tracer(c).start()

    def remote(src, dst, send, recv, to):
        return pltpu.make_async_remote_copy(src_ref=src, dst_ref=dst, send_sem=send, recv_sem=recv, device_id=to, device_id_type=MESH)

    def y_south(k, c):
        return remote(ystage.at[k, c, 0], yrecv.at[k, c, 1], ys_sem.at[k, c, 0], yr_sem.at[k, c, 1], south)

    def y_north(k, c):
        return remote(ystage.at[k, c, 1], yrecv.at[k, c, north_slot], ys_sem.at[k, c, 1], yr_sem.at[k, c, north_slot], north)

    def y_from(k, c, slot):
        return remote(ystage.at[k, c, slot], yrecv.at[k, c, slot], ys_sem.at[k, c, slot], yr_sem.at[k, c, slot], north)

    def x_west(k, c):
        return remote(xsend.at[k, c], xrecv.at[k, c, 1], xs_sem.at[k, c, 0], xr_sem.at[k, c, 1], west)

    def x_east(k, c):
        return remote(xsend.at[k, c], xrecv.at[k, c, 0], xs_sem.at[k, c, 1], xr_sem.at[k, c, 0], east)

    g_north = remote(gystage, gyrecv, g_sem.at[0], g_sem.at[1], north)
    g_east = remote(gxsend, gxrecv, g_sem.at[2], g_sem.at[3], east)

    def send_y(k, c):
        for f in range(NF):
            ystage[k, c, 0, pl.ds(2 * f, 2)] = F[k][c, f, pl.ds(BASE, 2)]
            ystage[k, c, 1, pl.ds(2 * f, 2)] = F[k][c, f, pl.ds(BASE + height - 2, 2)]

        @pl.when(top)
        def _():
            wide = (2 * NF, breadth)
            back = breadth - 1 - lax.broadcasted_iota(jnp.int32, wide, 1)
            row = lax.broadcasted_iota(jnp.int32, wide, 0)
            edge = jnp.take_along_axis(ystage[k, c, 1], back, axis=1)
            ystage[k, c, 1] = pick(lax.rem(row, 2) == 0, pltpu.roll(edge, 2 * NF - 1, 0), pltpu.roll(edge, 1, 0))

        @pl.when(inner)
        def _():
            y_south(k, c).start()

        y_north(k, c).start()

    def packed(values):
        found = pltpu.roll(values[0], 2, 1)
        for f in range(1, len(values)):
            found = pick(lane >= 4 * f, pltpu.roll(values[f], 2 + 4 * f, 1), found)
        return found

    def pack(source, target, fields, first, count):
        def tile(t, carry):
            at = first + 8 * t
            target[pl.ds(2 + at, 8)] = packed([source(f)[pl.ds(BASE + at, 8)] for f in range(fields)])
            return carry

        lax.fori_loop(0, count, tile, 0, unroll=4 if count % 4 == 0 else 3)

    def pack_rim(k, c):
        for at in (-2, height - 6):
            xsend[k, c, pl.ds(2 + at, 8)] = packed([F[k][c, f, pl.ds(BASE + at, 8)] for f in range(NF)])

    def send_x(k, c):
        y_from(k, c, 1).wait_recv()
        for f in range(NF):
            F[k][c, f, pl.ds(BASE + height, 2)] = yrecv[k, c, 1, pl.ds(2 * f, 2)]

        @pl.when(inner)
        def _():
            y_from(k, c, 0).wait_recv()
            for f in range(NF):
                F[k][c, f, pl.ds(BASE - 2, 2)] = yrecv[k, c, 0, pl.ds(2 * f, 2)]

        @pl.when(bottom)
        def _():
            for f in range(NF):
                F[k][c, f, pl.ds(BASE - 2, 2)] = jnp.zeros((2, breadth), jnp.float32)

        pack_rim(k, c)
        x_west(k, c).start()
        x_east(k, c).start()

    for copy in geo_loads:
        copy.wait()
    GF[2, inside] = CI[0].astype(jnp.float32)
    GF[3, inside] = CI[1].astype(jnp.float32)
    for f in range(4):
        gystage[pl.ds(f, 1)] = GF[f, pl.ds(BASE + height - 1, 1)]

    @pl.when(inner)
    def _():
        pl.semaphore_wait(barrier, 4)

    @pl.when(bottom)
    def _():
        pl.semaphore_wait(barrier, 3)

    @pl.when(jnp.logical_not(top))
    def _():
        g_north.start()

    block_rows = height // ice.shape[0]
    block_cols = breadth // ice.shape[1]

    def first(c, carry):
        load_mass(c).wait()
        load_tracer(c).wait()
        for r in range(ice.shape[0]):
            mask = jnp.zeros((block_rows, breadth), jnp.float32)
            wide = lax.broadcasted_iota(jnp.int32, (block_rows, breadth), 1)
            for q in range(ice.shape[1]):
                mask = pick(wide >= q * block_cols, ice[r, q].astype(jnp.float32), mask)
            band = pl.ds(BASE + r * block_rows, block_rows)
            FA[c, 0, band] = FA[c, 0, band] * mask
        send_y(0, c)
        return carry

    lax.fori_loop(0, ncat, first, 0)

    def columns(c, carry):
        pack(lambda f: FA.at[c, f], xsend.at[0, c], NF, 0, tiles)
        return carry

    lax.fori_loop(0, ncat, columns, 0)

    @pl.when(inner)
    def _():
        g_north.wait_recv()
        for f in range(4):
            GF[f, pl.ds(BASE - 1, 1)] = gyrecv[pl.ds(f, 1)]

    @pl.when(bottom)
    def _():
        for f in range(4):
            GF[f, pl.ds(BASE - 1, 1)] = jnp.zeros((1, breadth), jnp.float32)

    pack(lambda f: GF.at[f], gxsend, 4, -2, tiles + 1)
    g_east.start()

    def second(c, carry):
        send_x(0, c)
        return carry

    lax.fori_loop(0, ncat, second, 0)


    def save(where, at, values):
        for q, value in enumerate(values):
            where[q, at] = value

    def from_west(x, packed, f):
        return pltpu.roll(pick(lane == breadth - 1, pltpu.roll(packed, (breadth - 2 - 4 * f) % breadth, 1), x), 1, 1)

    def geometry(t, carry):
        here = pl.ds(pl.multiple_of(BASE + 8 * t, 8), 8)
        below = pl.ds(BASE - 1 + 8 * t, 8)
        at = pl.ds(pl.multiple_of(8 * t, 8), 8)
        u, v = GF[0, here], GF[1, here]
        u_below, v_below = GF[0, below], GF[1, below]
        save(GE, at, edge_geometry(0.5 * (u + u_below), jnp.abs(v_below), jnp.abs(v), GF[2, here]))
        return carry

    lax.fori_loop(0, tiles, geometry, 0, unroll=2)
    g_east.wait_recv()

    def west_geometry(t, carry):
        here = pl.ds(pl.multiple_of(BASE + 8 * t, 8), 8)
        below = pl.ds(BASE - 1 + 8 * t, 8)
        at = pl.ds(pl.multiple_of(8 * t, 8), 8)
        u, v = GF[0, here], GF[1, here]
        u_below, v_below = GF[0, below], GF[1, below]
        mine, lower = gxrecv[pl.ds(2 + 8 * t, 8)], gxrecv[pl.ds(1 + 8 * t, 8)]
        u, u_below = from_west(u, mine, 0), from_west(u_below, lower, 0)
        v, v_below = from_west(v, mine, 1), from_west(v_below, lower, 1)
        save(GW, at, edge_geometry(0.5 * (u + u_below), jnp.abs(v_below), jnp.abs(v), from_west(GF[2, here], mine, 2)))
        return carry

    lax.fori_loop(0, tiles, west_geometry, 0, unroll=2)

    def north_geometry(t, carry):
        start = jnp.minimum(8 * t - 1, height - 8)
        here = pl.ds(BASE + start, 8)
        u, v, packed = GF[0, here], GF[1, here], gxrecv[pl.ds(2 + start, 8)]

        u_west, v_west = from_west(u, packed, 0), from_west(v, packed, 1)
        save(GN, here, edge_geometry(0.5 * (v + v_west), jnp.abs(u_west), jnp.abs(u), GF[3, here]))
        return carry

    lax.fori_loop(0, tiles + 1, north_geometry, 0, unroll=3)

    def edges(where, at):
        a, area, x1, x2, off, case = (where[q, at] for q in range(6))
        return a, area, x1, x2, off, a > 0.0, case == 2.0

    edge_lanes = (lane >= breadth - 2, lane >= breadth - 1, lane < 1, lane < 2)
    left = lax.rem(lane, 4) < 2

    def shift_tile(k, c, S, t):
        at = pl.ds(8 * t if isinstance(t, int) else pl.multiple_of(8 * t, 8), 8)
        halo = pick(left, xrecv[k, c, 0, at], xrecv[k, c, 1, at])

        def piece(f):
            value = F[k][c, f, pl.ds(BASE - 2 + 8 * t, 8)]
            side = pltpu.roll(halo, (breadth - 2 - 4 * f) % breadth, 1)
            for q, shift in enumerate(SHIFTS):
                S[q, f, at] = pltpu.roll(pick(edge_lanes[q], side, value), -shift % breadth, 1)

        return [functools.partial(piece, f) for f in range(NF)]

    def advance(k, c, S, ahead, between):
        def reader(f, start):
            def get(row, col):
                if col == 0:
                    return F[k][c, f, pl.ds(BASE + start + row, 8)]
                return S[SHIFTS.index(col), f, pl.ds(2 + start + row, 8)]

            return remember(get)

        def north_edges(get, start):
            at = pl.ds(BASE + start, 8)
            flux, points = mass_flux(get, edges(GN, at))
            ND[0, at] = flux
            for q, (value, _) in enumerate(points.values()):
                ND[1 + q, at] = value
            return flux, points

        north_edges(reader(0, -1), -1)
        for work in ahead(tiles):
            work()

        def tile(t, carry):
            start = pl.multiple_of(8 * t, 8)
            at = pl.ds(start, 8)
            after = pl.ds(BASE + start, 8)
            before = pl.ds(BASE - 1 + start, 8)
            work = ahead(t)
            get = reader(0, start)
            mass = get(0, 0)
            north, north_points = north_edges(get, start)
            if work:
                work[0]()
            east, east_points = mass_flux(lambda n, t: get(t, n), edges(GE, at))
            west, west_points = mass_flux(lambda n, t: get(t, n - 1), edges(GW, at))
            total = {(0, 0): mass}

            def emit(f, value):
                if k + 1 < STEPS:
                    F[k + 1][c, f, after] = value
                elif f:
                    tracer_out[c, f - 1, at] = value
                else:
                    mass_out[c, at] = value


            def add(where, value, sign):
                if where not in total:
                    total[where] = value if sign > 0 else -value
                elif sign > 0:
                    total[where] = total[where] + value
                else:
                    total[where] = total[where] - value

            for (n, q), (value, sign) in west_points.items():
                add((q, n - 1), value, sign)
            for i, ((n, q), (_, sign)) in enumerate(north_points.items()):
                add((n - 1, q), ND[1 + i, before], sign)
            for (n, q), (value, sign) in east_points.items():
                add((q, n), value, -sign)
            for (n, q), (value, sign) in north_points.items():
                add((n, q), value, -sign)
            new_mass = mass - (east - west) - (north - ND[0, before])
            emit(0, new_mass)
            scale = 1.0 / jnp.maximum(new_mass, FLOOR)
            for f in range(1, NF):
                if work:
                    work[f]()
                get = reader(f, start)
                sums = [None, None]
                for i, ((row, col), value) in enumerate(total.items()):
                    term = value * get(row, col)
                    sums[i % 2] = term if sums[i % 2] is None else sums[i % 2] + term
                emit(f, (sums[0] + sums[1]) * scale)
            return carry

        if between is None:
            lax.fori_loop(0, tiles, tile, 0)
        else:
            lax.fori_loop(0, tiles // 2, tile, 0)
            send_x(1, between)
            lax.fori_loop(tiles // 2, tiles, tile, 0)
        if k + 1 < STEPS:
            pack(lambda f: F[k + 1].at[c, f], xsend.at[k + 1, c], NF, 0, tiles)

    def x_wait(k, c):
        x_east(k, c).wait_recv()
        x_west(k, c).wait_recv()

    order = [(k, c) for k in range(STEPS) for c in range(ncat)]
    x_wait(0, 0)

    def whole(t, carry):
        for work in shift_tile(0, 0, SA, t):
            work()
        return carry

    lax.fori_loop(0, tiles + 1, whole, 0, unroll=3)
    for i, (k, c) in enumerate(order):
        if i + 1 < ncat:
            x_wait(*order[i + 1])
            ahead = functools.partial(shift_tile, *order[i + 1], (SA, SB)[(i + 1) % 2])
        else:
            ahead = lambda t: []
        advance(k, c, (SA, SB)[i % 2], ahead, None)
        if 2 <= i < ncat + 2:
            send_x(1, i - 2)
        if ncat <= i + 1 < len(order):
            x_wait(*order[i + 1])
            nxt = order[i + 1]

            def whole(t, carry, nxt=nxt, S=(SA, SB)[(i + 1) % 2]):
                for work in shift_tile(*nxt, S, t):
                    work()
                return carry

            lax.fori_loop(0, tiles + 1, whole, 0, unroll=3)
        if k == 0:
            send_y(1, c)

    @pl.when(jnp.logical_not(top))
    def _():
        g_north.wait_send()

    g_east.wait_send()

    def finish(c, carry):
        for k in range(STEPS):
            @pl.when(inner)
            def _():
                y_south(k, c).wait_send()

            y_north(k, c).wait_send()
            x_west(k, c).wait_send()
            x_east(k, c).wait_send()
        return carry

    lax.fori_loop(0, ncat, finish, 0)


def solution(mesh):
    nx, ny = mesh.shape["gx"], mesh.shape["gy"]

    def per_device(mass, tracer, uvel, vvel, case_east, case_north, ice):
        ncat, height, breadth = mass.shape
        rows = height + 2 * BASE
        packed = height + 8
        f32 = jnp.float32
        hbm = pl.BlockSpec(memory_space=pl.ANY)
        return pl.pallas_call(
            functools.partial(kernel, nx, ny, ncat, height, breadth),
            out_shape=(pltpu.VMEM(mass.shape, f32), pltpu.VMEM(tracer.shape, f32)),
            in_specs=[hbm] * 6 + [pl.BlockSpec(memory_space=pltpu.SMEM)],
            out_specs=(pl.BlockSpec(memory_space=pltpu.VMEM),) * 2,
            scratch_shapes=[
                pltpu.VMEM((ncat, NF, rows, breadth), f32),
                pltpu.VMEM((ncat, NF, rows, breadth), f32),
                pltpu.VMEM((4, NF, packed, breadth), f32),
                pltpu.VMEM((4, NF, packed, breadth), f32),
                pltpu.VMEM((17, packed, breadth), f32),
                pltpu.VMEM((4, rows, breadth), f32),
                pltpu.VMEM((2, height, breadth), jnp.int32),
                pltpu.VMEM((6, height, breadth), f32),
                pltpu.VMEM((6, packed, breadth), f32),
                pltpu.VMEM((6, height, breadth), f32),
                pltpu.VMEM((STEPS, ncat, 2, 2 * NF, breadth), f32),
                pltpu.VMEM((STEPS, ncat, 2, 2 * NF, breadth), f32),
                pltpu.VMEM((STEPS, ncat, packed, breadth), f32),
                pltpu.VMEM((STEPS, ncat, 2, packed, breadth), f32),
                pltpu.VMEM((8, breadth), f32),
                pltpu.VMEM((8, breadth), f32),
                pltpu.VMEM((packed, breadth), f32),
                pltpu.VMEM((packed, breadth), f32),
                pltpu.SemaphoreType.DMA((3, max(ncat, 4))),
                pltpu.SemaphoreType.DMA((STEPS, ncat, 2)),
                pltpu.SemaphoreType.DMA((STEPS, ncat, 2)),
                pltpu.SemaphoreType.DMA((STEPS, ncat, 2)),
                pltpu.SemaphoreType.DMA((STEPS, ncat, 2)),
                pltpu.SemaphoreType.DMA((4,)),
            ],
            compiler_params=pltpu.CompilerParams(collective_id=0, has_side_effects=True),
        )(mass, tracer, uvel, vvel, case_east, case_north, ice)

    placed = (P(None, "gy", "gx"), P(None, None, "gy", "gx")) + (P("gy", "gx"),) * 5
    return jax.shard_map(
        per_device,
        mesh=mesh,
        in_specs=placed,
        out_specs=(P(None, "gy", "gx"), P(None, None, "gy", "gx")),
        check_vma=False,
    )
```

```python
import functools

import jax
import jax.numpy as jnp
from jax import lax
from jax.experimental import pallas as pl
from jax.experimental.pallas import tpu as pltpu
from jax.sharding import PartitionSpec as P

STEPS = 2
NF = 8
FLOOR = 0.1
SHIFTS = (-2, -1, 1, 2)
MESH = pl.DeviceIdType.MESH
BASE = 8
pick = jnp.where


def oriented(get, s, d):
    near = [pick(d, get(n, 1), get(n, -1)) for n in (-1, 0, 1, 2)]
    far = [pick(d, get(n, -1), get(n, 1)) for n in (0, 1)]
    two = [pick(d, get(n, 2), get(n, -2)) for n in (0, 1)]
    h = pick(s, get(0, 0), get(1, 0))
    b = pick(s, get(1, 0), get(0, 0))
    c = pick(s, get(-1, 0), get(2, 0))
    hd = pick(s, near[1], near[2])
    bd = pick(s, near[2], near[1])
    cd = pick(s, near[0], near[3])
    return h, b, c, hd, bd, cd, pick(s, far[0], far[1]), pick(s, two[0], two[1])


def mass_flux(get, geo):
    a, area, x1, x2, off, s, d = geo
    h, b, c, hd, bd, cd, hm, h2 = oriented(get, s, d)
    g = b - c
    w1 = a * (h + g * x1)
    w2 = area * (h + g * x2 + (hd - hm) * off)
    w3 = area * (hd + (bd - cd) * x2 - (h2 - h) * off)
    w2o = w2 * off
    w3o = w3 * off
    flux = w1 - w2 + w3
    ch = w1 - w2 + w3o
    cb = w1 * x1 - w2 * x2
    chd = w3 - w2o
    cbd = w3 * x2
    zero = jnp.zeros_like(flux)
    points = {
        (0, 0): (pick(s, ch, cb), 1),
        (1, 0): (pick(s, cb, ch), 1),
        (-1, 0): (pick(s, cb, zero), -1),
        (2, 0): (pick(s, zero, cb), -1),
    }
    e0, e1 = pick(s, chd, cbd), pick(s, cbd, chd)
    back0, back1 = pick(s, w2o, zero), pick(s, zero, w2o)
    behind, beyond = pick(s, cbd, zero), pick(s, zero, cbd)
    far0, far1 = pick(s, w3o, zero), pick(s, zero, w3o)
    points[0, 1], points[0, -1] = (pick(d, e0, back0), 1), (pick(d, back0, e0), 1)
    points[1, 1], points[1, -1] = (pick(d, e1, back1), 1), (pick(d, back1, e1), 1)
    points[-1, 1], points[-1, -1] = (pick(d, behind, zero), -1), (pick(d, zero, behind), -1)
    points[2, 1], points[2, -1] = (pick(d, beyond, zero), -1), (pick(d, zero, beyond), -1)
    points[0, 2], points[0, -2] = (pick(d, far0, zero), -1), (pick(d, zero, far0), -1)
    points[1, 2], points[1, -2] = (pick(d, far1, zero), -1), (pick(d, zero, far1), -1)
    return flux, points


def edge_geometry(a, low, high, case):
    reach = jnp.abs(a)
    b = pick(case == 2.0, high, low)
    area = pick(case == 0.0, 0.0, 0.5 * a * b)
    return a, area, 0.25 - 0.25 * reach, 0.25 - reach / 6.0, 0.25 - b / 6.0, case


def remember(get):
    seen = {}

    def load(n, t):
        if (n, t) not in seen:
            seen[n, t] = get(n, t)
        return seen[n, t]

    return load


def kernel(nx, ny, ncat, height, breadth,
           mass_hbm, tracer_hbm, u_hbm, v_hbm, ce_hbm, cn_hbm, ice,
           mass_out, tracer_out,
           FA, FB, SA, SB, ND, GF, CI, GE, GN, GW,
           ystage, yrecv, xsend, xrecv, gystage, gyrecv, gxsend, gxrecv,
           in_sem, ys_sem, yr_sem, xs_sem, xr_sem, g_sem):
    F = (FA, FB)
    gx = lax.axis_index("gx")
    gy = lax.axis_index("gy")
    bottom = gy == 0
    top = gy == ny - 1
    inner = gy > 0
    west = {"gx": lax.rem(gx + nx - 1, nx), "gy": gy}
    east = {"gx": lax.rem(gx + 1, nx), "gy": gy}
    south = {"gx": gx, "gy": jnp.maximum(gy - 1, 0)}
    north = {"gx": pick(top, nx - 1 - gx, gx), "gy": pick(top, gy, gy + 1)}
    north_slot = pick(top, 1, 0)
    tiles = height // 8
    rows = height + 2 * BASE
    inside = pl.ds(BASE, height)
    lane = lax.broadcasted_iota(jnp.int32, (8, breadth), 1)

    barrier = pltpu.get_barrier_semaphore()
    for where in (west, east, north):
        pl.semaphore_signal(barrier, inc=1, device_id=where, device_id_type=MESH)

    @pl.when(inner)
    def _():
        pl.semaphore_signal(barrier, inc=1, device_id=south, device_id_type=MESH)

    def load_mass(c):
        return pltpu.make_async_copy(mass_hbm.at[c], FA.at[c, 0, inside], in_sem.at[0, c])

    def load_tracer(c):
        return pltpu.make_async_copy(tracer_hbm.at[c], FA.at[c, pl.ds(1, NF - 1), inside], in_sem.at[1, c])

    geo_loads = [
        pltpu.make_async_copy(u_hbm, GF.at[0, inside], in_sem.at[2, 0]),
        pltpu.make_async_copy(v_hbm, GF.at[1, inside], in_sem.at[2, 1]),
        pltpu.make_async_copy(ce_hbm, CI.at[0], in_sem.at[2, 2]),
        pltpu.make_async_copy(cn_hbm, CI.at[1], in_sem.at[2, 3]),
    ]
    for copy in geo_loads:
        copy.start()
    for c in range(ncat):
        load_mass(c).start()
        load_tracer(c).start()

    def remote(src, dst, send, recv, to):
        return pltpu.make_async_remote_copy(src_ref=src, dst_ref=dst, send_sem=send, recv_sem=recv, device_id=to, device_id_type=MESH)

    def y_south(k, c):
        return remote(ystage.at[k, c, 0], yrecv.at[k, c, 1], ys_sem.at[k, c, 0], yr_sem.at[k, c, 1], south)

    def y_north(k, c):
        return remote(ystage.at[k, c, 1], yrecv.at[k, c, north_slot], ys_sem.at[k, c, 1], yr_sem.at[k, c, north_slot], north)

    def y_from(k, c, slot):
        return remote(ystage.at[k, c, slot], yrecv.at[k, c, slot], ys_sem.at[k, c, slot], yr_sem.at[k, c, slot], north)

    def x_west(k, c):
        return remote(xsend.at[k, c], xrecv.at[k, c, 1], xs_sem.at[k, c, 0], xr_sem.at[k, c, 1], west)

    def x_east(k, c):
        return remote(xsend.at[k, c], xrecv.at[k, c, 0], xs_sem.at[k, c, 1], xr_sem.at[k, c, 0], east)

    g_north = remote(gystage, gyrecv, g_sem.at[0], g_sem.at[1], north)
    g_east = remote(gxsend, gxrecv, g_sem.at[2], g_sem.at[3], east)

    def send_y(k, c):
        for f in range(NF):
            ystage[k, c, 0, pl.ds(2 * f, 2)] = F[k][c, f, pl.ds(BASE, 2)]
            ystage[k, c, 1, pl.ds(2 * f, 2)] = F[k][c, f, pl.ds(BASE + height - 2, 2)]

        @pl.when(top)
        def _():
            wide = (2 * NF, breadth)
            back = breadth - 1 - lax.broadcasted_iota(jnp.int32, wide, 1)
            row = lax.broadcasted_iota(jnp.int32, wide, 0)
            edge = jnp.take_along_axis(ystage[k, c, 1], back, axis=1)
            ystage[k, c, 1] = pick(lax.rem(row, 2) == 0, pltpu.roll(edge, 2 * NF - 1, 0), pltpu.roll(edge, 1, 0))

        @pl.when(inner)
        def _():
            y_south(k, c).start()

        y_north(k, c).start()

    def packed(values):
        found = pltpu.roll(values[0], 2, 1)
        for f in range(1, len(values)):
            found = pick(lane >= 4 * f, pltpu.roll(values[f], 2 + 4 * f, 1), found)
        return found

    def pack(source, target, fields, first, count):
        def tile(t, carry):
            at = first + 8 * t
            target[pl.ds(2 + at, 8)] = packed([source(f)[pl.ds(BASE + at, 8)] for f in range(fields)])
            return carry

        lax.fori_loop(0, count, tile, 0, unroll=4 if count % 4 == 0 else 3)

    def pack_rim(k, c):
        for at in (-2, height - 6):
            xsend[k, c, pl.ds(2 + at, 8)] = packed([F[k][c, f, pl.ds(BASE + at, 8)] for f in range(NF)])

    def send_x(k, c):
        y_from(k, c, 1).wait_recv()
        for f in range(NF):
            F[k][c, f, pl.ds(BASE + height, 2)] = yrecv[k, c, 1, pl.ds(2 * f, 2)]

        @pl.when(inner)
        def _():
            y_from(k, c, 0).wait_recv()
            for f in range(NF):
                F[k][c, f, pl.ds(BASE - 2, 2)] = yrecv[k, c, 0, pl.ds(2 * f, 2)]

        @pl.when(bottom)
        def _():
            for f in range(NF):
                F[k][c, f, pl.ds(BASE - 2, 2)] = jnp.zeros((2, breadth), jnp.float32)

        pack_rim(k, c)
        x_west(k, c).start()
        x_east(k, c).start()

    for copy in geo_loads:
        copy.wait()
    GF[2, inside] = CI[0].astype(jnp.float32)
    GF[3, inside] = CI[1].astype(jnp.float32)
    for f in range(4):
        gystage[pl.ds(f, 1)] = GF[f, pl.ds(BASE + height - 1, 1)]

    @pl.when(inner)
    def _():
        pl.semaphore_wait(barrier, 4)

    @pl.when(bottom)
    def _():
        pl.semaphore_wait(barrier, 3)

    @pl.when(jnp.logical_not(top))
    def _():
        g_north.start()

    block_rows = height // ice.shape[0]
    block_cols = breadth // ice.shape[1]

    def first(c, carry):
        load_mass(c).wait()
        load_tracer(c).wait()
        for r in range(ice.shape[0]):
            mask = jnp.zeros((block_rows, breadth), jnp.float32)
            wide = lax.broadcasted_iota(jnp.int32, (block_rows, breadth), 1)
            for q in range(ice.shape[1]):
                mask = pick(wide >= q * block_cols, ice[r, q].astype(jnp.float32), mask)
            band = pl.ds(BASE + r * block_rows, block_rows)
            FA[c, 0, band] = FA[c, 0, band] * mask
        send_y(0, c)
        return carry

    lax.fori_loop(0, ncat, first, 0)

    def columns(c, carry):
        pack(lambda f: FA.at[c, f], xsend.at[0, c], NF, 0, tiles)
        return carry

    lax.fori_loop(0, ncat, columns, 0)

    @pl.when(inner)
    def _():
        g_north.wait_recv()
        for f in range(4):
            GF[f, pl.ds(BASE - 1, 1)] = gyrecv[pl.ds(f, 1)]

    @pl.when(bottom)
    def _():
        for f in range(4):
            GF[f, pl.ds(BASE - 1, 1)] = jnp.zeros((1, breadth), jnp.float32)

    pack(lambda f: GF.at[f], gxsend, 4, -2, tiles + 1)
    g_east.start()

    def second(c, carry):
        send_x(0, c)
        return carry

    lax.fori_loop(0, ncat, second, 0)


    def save(where, at, values):
        for q, value in enumerate(values):
            where[q, at] = value

    def from_west(x, packed, f):
        return pltpu.roll(pick(lane == breadth - 1, pltpu.roll(packed, (breadth - 2 - 4 * f) % breadth, 1), x), 1, 1)

    def geometry(t, carry):
        here = pl.ds(pl.multiple_of(BASE + 8 * t, 8), 8)
        below = pl.ds(BASE - 1 + 8 * t, 8)
        at = pl.ds(pl.multiple_of(8 * t, 8), 8)
        u, v = GF[0, here], GF[1, here]
        u_below, v_below = GF[0, below], GF[1, below]
        save(GE, at, edge_geometry(0.5 * (u + u_below), jnp.abs(v_below), jnp.abs(v), GF[2, here]))
        return carry

    lax.fori_loop(0, tiles, geometry, 0, unroll=2)
    g_east.wait_recv()

    def west_geometry(t, carry):
        here = pl.ds(pl.multiple_of(BASE + 8 * t, 8), 8)
        below = pl.ds(BASE - 1 + 8 * t, 8)
        at = pl.ds(pl.multiple_of(8 * t, 8), 8)
        u, v = GF[0, here], GF[1, here]
        u_below, v_below = GF[0, below], GF[1, below]
        mine, lower = gxrecv[pl.ds(2 + 8 * t, 8)], gxrecv[pl.ds(1 + 8 * t, 8)]
        u, u_below = from_west(u, mine, 0), from_west(u_below, lower, 0)
        v, v_below = from_west(v, mine, 1), from_west(v_below, lower, 1)
        save(GW, at, edge_geometry(0.5 * (u + u_below), jnp.abs(v_below), jnp.abs(v), from_west(GF[2, here], mine, 2)))
        return carry

    lax.fori_loop(0, tiles, west_geometry, 0, unroll=2)

    def north_geometry(t, carry):
        start = jnp.minimum(8 * t - 1, height - 8)
        here = pl.ds(BASE + start, 8)
        u, v, packed = GF[0, here], GF[1, here], gxrecv[pl.ds(2 + start, 8)]

        u_west, v_west = from_west(u, packed, 0), from_west(v, packed, 1)
        save(GN, here, edge_geometry(0.5 * (v + v_west), jnp.abs(u_west), jnp.abs(u), GF[3, here]))
        return carry

    lax.fori_loop(0, tiles + 1, north_geometry, 0, unroll=3)

    def edges(where, at):
        a, area, x1, x2, off, case = (where[q, at] for q in range(6))
        return a, area, x1, x2, off, a > 0.0, case == 2.0

    edge_lanes = (lane >= breadth - 2, lane >= breadth - 1, lane < 1, lane < 2)
    left = lax.rem(lane, 4) < 2

    def shift_tile(k, c, S, t):
        at = pl.ds(8 * t if isinstance(t, int) else pl.multiple_of(8 * t, 8), 8)
        halo = pick(left, xrecv[k, c, 0, at], xrecv[k, c, 1, at])

        def piece(f):
            value = F[k][c, f, pl.ds(BASE - 2 + 8 * t, 8)]
            side = pltpu.roll(halo, (breadth - 2 - 4 * f) % breadth, 1)
            for q, shift in enumerate(SHIFTS):
                S[q, f, at] = pltpu.roll(pick(edge_lanes[q], side, value), -shift % breadth, 1)

        return [functools.partial(piece, f) for f in range(NF)]

    def advance(k, c, S, ahead):
        def reader(f, start):
            def get(row, col):
                if col == 0:
                    return F[k][c, f, pl.ds(BASE + start + row, 8)]
                return S[SHIFTS.index(col), f, pl.ds(2 + start + row, 8)]

            return remember(get)

        def north_edges(get, start):
            at = pl.ds(BASE + start, 8)
            flux, points = mass_flux(get, edges(GN, at))
            ND[0, at] = flux
            for q, (value, _) in enumerate(points.values()):
                ND[1 + q, at] = value
            return flux, points

        north_edges(reader(0, -1), -1)
        for work in ahead(tiles):
            work()

        def tile(t, carry):
            start = pl.multiple_of(8 * t, 8)
            at = pl.ds(start, 8)
            after = pl.ds(BASE + start, 8)
            before = pl.ds(BASE - 1 + start, 8)
            work = ahead(t)
            get = reader(0, start)
            mass = get(0, 0)
            north, north_points = north_edges(get, start)
            if work:
                work[0]()
            east, east_points = mass_flux(lambda n, t: get(t, n), edges(GE, at))
            west, west_points = mass_flux(lambda n, t: get(t, n - 1), edges(GW, at))
            total = {(0, 0): mass}

            def emit(f, value):
                if k + 1 < STEPS:
                    F[k + 1][c, f, after] = value
                elif f:
                    tracer_out[c, f - 1, at] = value
                else:
                    mass_out[c, at] = value


            def add(where, value, sign):
                if where not in total:
                    total[where] = value if sign > 0 else -value
                elif sign > 0:
                    total[where] = total[where] + value
                else:
                    total[where] = total[where] - value

            for (n, q), (value, sign) in west_points.items():
                add((q, n - 1), value, sign)
            for i, ((n, q), (_, sign)) in enumerate(north_points.items()):
                add((n - 1, q), ND[1 + i, before], sign)
            for (n, q), (value, sign) in east_points.items():
                add((q, n), value, -sign)
            for (n, q), (value, sign) in north_points.items():
                add((n, q), value, -sign)
            new_mass = mass - (east - west) - (north - ND[0, before])
            emit(0, new_mass)
            scale = 1.0 / jnp.maximum(new_mass, FLOOR)
            for f in range(1, NF):
                if work:
                    work[f]()
                get = reader(f, start)
                sums = [None, None]
                for i, ((row, col), value) in enumerate(total.items()):
                    term = value * get(row, col)
                    sums[i % 2] = term if sums[i % 2] is None else sums[i % 2] + term
                emit(f, (sums[0] + sums[1]) * scale)
            return carry

        if k + 1 < STEPS:
            north_edges(reader(0, height - 9), height - 9)
            lax.fori_loop(0, 2, lambda i, carry: tile((tiles - 1) * i, carry), 0)
            send_y(k + 1, c)
            lax.fori_loop(1, tiles - 1, tile, 0)
        else:
            lax.fori_loop(0, tiles, tile, 0, unroll=1 if ahead(0) else 4)

    def x_wait(k, c):
        x_east(k, c).wait_recv()
        x_west(k, c).wait_recv()

    order = [(k, c) for k in range(STEPS) for c in range(ncat)]
    x_wait(0, 0)

    def whole(t, carry):
        for work in shift_tile(0, 0, SA, t):
            work()
        return carry

    lax.fori_loop(0, tiles + 1, whole, 0, unroll=3)
    for i, (k, c) in enumerate(order):
        if i + 1 < ncat:
            x_wait(*order[i + 1])
            ahead = functools.partial(shift_tile, *order[i + 1], (SA, SB)[(i + 1) % 2])
        else:
            ahead = lambda t: []
        advance(k, c, (SA, SB)[i % 2], ahead)
        if 2 <= i < ncat + 2:
            send_x(1, i - 2)
        if ncat <= i + 1 < len(order):
            x_wait(*order[i + 1])
            nxt = order[i + 1]

            def whole(t, carry, nxt=nxt, S=(SA, SB)[(i + 1) % 2]):
                for work in shift_tile(*nxt, S, t):
                    work()
                return carry

            lax.fori_loop(0, tiles + 1, whole, 0, unroll=3)
        if k == 0:
            pack(lambda f: FB.at[c, f], xsend.at[1, c], NF, 0, tiles)

    @pl.when(jnp.logical_not(top))
    def _():
        g_north.wait_send()

    g_east.wait_send()

    def finish(c, carry):
        for k in range(STEPS):
            @pl.when(inner)
            def _():
                y_south(k, c).wait_send()

            y_north(k, c).wait_send()
            x_west(k, c).wait_send()
            x_east(k, c).wait_send()
        return carry

    lax.fori_loop(0, ncat, finish, 0)


def solution(mesh):
    nx, ny = mesh.shape["gx"], mesh.shape["gy"]

    def per_device(mass, tracer, uvel, vvel, case_east, case_north, ice):
        ncat, height, breadth = mass.shape
        rows = height + 2 * BASE
        packed = height + 8
        f32 = jnp.float32
        hbm = pl.BlockSpec(memory_space=pl.ANY)
        return pl.pallas_call(
            functools.partial(kernel, nx, ny, ncat, height, breadth),
            out_shape=(pltpu.VMEM(mass.shape, f32), pltpu.VMEM(tracer.shape, f32)),
            in_specs=[hbm] * 6 + [pl.BlockSpec(memory_space=pltpu.SMEM)],
            out_specs=(pl.BlockSpec(memory_space=pltpu.VMEM),) * 2,
            scratch_shapes=[
                pltpu.VMEM((ncat, NF, rows, breadth), f32),
                pltpu.VMEM((ncat, NF, rows, breadth), f32),
                pltpu.VMEM((4, NF, packed, breadth), f32),
                pltpu.VMEM((4, NF, packed, breadth), f32),
                pltpu.VMEM((17, packed, breadth), f32),
                pltpu.VMEM((4, rows, breadth), f32),
                pltpu.VMEM((2, height, breadth), jnp.int32),
                pltpu.VMEM((6, height, breadth), f32),
                pltpu.VMEM((6, packed, breadth), f32),
                pltpu.VMEM((6, height, breadth), f32),
                pltpu.VMEM((STEPS, ncat, 2, 2 * NF, breadth), f32),
                pltpu.VMEM((STEPS, ncat, 2, 2 * NF, breadth), f32),
                pltpu.VMEM((STEPS, ncat, packed, breadth), f32),
                pltpu.VMEM((STEPS, ncat, 2, packed, breadth), f32),
                pltpu.VMEM((8, breadth), f32),
                pltpu.VMEM((8, breadth), f32),
                pltpu.VMEM((packed, breadth), f32),
                pltpu.VMEM((packed, breadth), f32),
                pltpu.SemaphoreType.DMA((3, max(ncat, 4))),
                pltpu.SemaphoreType.DMA((STEPS, ncat, 2)),
                pltpu.SemaphoreType.DMA((STEPS, ncat, 2)),
                pltpu.SemaphoreType.DMA((STEPS, ncat, 2)),
                pltpu.SemaphoreType.DMA((STEPS, ncat, 2)),
                pltpu.SemaphoreType.DMA((4,)),
            ],
            compiler_params=pltpu.CompilerParams(collective_id=0, has_side_effects=True),
        )(mass, tracer, uvel, vvel, case_east, case_north, ice)

    placed = (P(None, "gy", "gx"), P(None, None, "gy", "gx")) + (P("gy", "gx"),) * 5
    return jax.shard_map(
        per_device,
        mesh=mesh,
        in_specs=placed,
        out_specs=(P(None, "gy", "gx"), P(None, None, "gy", "gx")),
        check_vma=False,
    )
```

```python
import functools

import jax
import jax.numpy as jnp
from jax import lax
from jax.experimental import pallas as pl
from jax.experimental.pallas import tpu as pltpu
from jax.sharding import PartitionSpec as P

STEPS = 2
NF = 8
FLOOR = 0.1
SHIFTS = (-2, -1, 1, 2)
MESH = pl.DeviceIdType.MESH
BASE = 8
pick = jnp.where


def oriented(get, s, d):
    near = [pick(d, get(n, 1), get(n, -1)) for n in (-1, 0, 1, 2)]
    far = [pick(d, get(n, -1), get(n, 1)) for n in (0, 1)]
    two = [pick(d, get(n, 2), get(n, -2)) for n in (0, 1)]
    h = pick(s, get(0, 0), get(1, 0))
    b = pick(s, get(1, 0), get(0, 0))
    c = pick(s, get(-1, 0), get(2, 0))
    hd = pick(s, near[1], near[2])
    bd = pick(s, near[2], near[1])
    cd = pick(s, near[0], near[3])
    return h, b, c, hd, bd, cd, pick(s, far[0], far[1]), pick(s, two[0], two[1])


def mass_flux(get, geo):
    a, area, x1, x2, off, s, d = geo
    h, b, c, hd, bd, cd, hm, h2 = oriented(get, s, d)
    g = b - c
    w1 = a * (h + g * x1)
    w2 = area * (h + g * x2 + (hd - hm) * off)
    w3 = area * (hd + (bd - cd) * x2 - (h2 - h) * off)
    w2o = w2 * off
    w3o = w3 * off
    flux = w1 - w2 + w3
    ch = w1 - w2 + w3o
    cb = w1 * x1 - w2 * x2
    chd = w3 - w2o
    cbd = w3 * x2
    zero = jnp.zeros_like(flux)
    points = {
        (0, 0): (pick(s, ch, cb), 1),
        (1, 0): (pick(s, cb, ch), 1),
        (-1, 0): (pick(s, cb, zero), -1),
        (2, 0): (pick(s, zero, cb), -1),
    }
    e0, e1 = pick(s, chd, cbd), pick(s, cbd, chd)
    back0, back1 = pick(s, w2o, zero), pick(s, zero, w2o)
    behind, beyond = pick(s, cbd, zero), pick(s, zero, cbd)
    far0, far1 = pick(s, w3o, zero), pick(s, zero, w3o)
    points[0, 1], points[0, -1] = (pick(d, e0, back0), 1), (pick(d, back0, e0), 1)
    points[1, 1], points[1, -1] = (pick(d, e1, back1), 1), (pick(d, back1, e1), 1)
    points[-1, 1], points[-1, -1] = (pick(d, behind, zero), -1), (pick(d, zero, behind), -1)
    points[2, 1], points[2, -1] = (pick(d, beyond, zero), -1), (pick(d, zero, beyond), -1)
    points[0, 2], points[0, -2] = (pick(d, far0, zero), -1), (pick(d, zero, far0), -1)
    points[1, 2], points[1, -2] = (pick(d, far1, zero), -1), (pick(d, zero, far1), -1)
    return flux, points


def edge_geometry(a, low, high, case):
    reach = jnp.abs(a)
    b = pick(case == 2.0, high, low)
    area = pick(case == 0.0, 0.0, 0.5 * a * b)
    return a, area, 0.25 - 0.25 * reach, 0.25 - reach / 6.0, 0.25 - b / 6.0, case


def remember(get):
    seen = {}

    def load(n, t):
        if (n, t) not in seen:
            seen[n, t] = get(n, t)
        return seen[n, t]

    return load


def kernel(nx, ny, ncat, height, breadth,
           mass_hbm, tracer_hbm, u_hbm, v_hbm, ce_hbm, cn_hbm, ice,
           mass_out, tracer_out,
           FA, FB, SA, SB, ND, GF, CI, GE, GN, GW,
           ystage, yrecv, xsend, xrecv, gystage, gyrecv, gxsend, gxrecv,
           in_sem, ys_sem, yr_sem, xs_sem, xr_sem, g_sem):
    F = (FA, FB)
    gx = lax.axis_index("gx")
    gy = lax.axis_index("gy")
    bottom = gy == 0
    top = gy == ny - 1
    inner = gy > 0
    west = {"gx": lax.rem(gx + nx - 1, nx), "gy": gy}
    east = {"gx": lax.rem(gx + 1, nx), "gy": gy}
    south = {"gx": gx, "gy": jnp.maximum(gy - 1, 0)}
    north = {"gx": pick(top, nx - 1 - gx, gx), "gy": pick(top, gy, gy + 1)}
    north_slot = pick(top, 1, 0)
    tiles = height // 8
    rows = height + 2 * BASE
    inside = pl.ds(BASE, height)
    lane = lax.broadcasted_iota(jnp.int32, (8, breadth), 1)

    barrier = pltpu.get_barrier_semaphore()
    for where in (west, east, north):
        pl.semaphore_signal(barrier, inc=1, device_id=where, device_id_type=MESH)

    @pl.when(inner)
    def _():
        pl.semaphore_signal(barrier, inc=1, device_id=south, device_id_type=MESH)

    def load_mass(c):
        return pltpu.make_async_copy(mass_hbm.at[c], FA.at[c, 0, inside], in_sem.at[0, c])

    def load_tracer(c):
        return pltpu.make_async_copy(tracer_hbm.at[c], FA.at[c, pl.ds(1, NF - 1), inside], in_sem.at[1, c])

    geo_loads = [
        pltpu.make_async_copy(u_hbm, GF.at[0, inside], in_sem.at[2, 0]),
        pltpu.make_async_copy(v_hbm, GF.at[1, inside], in_sem.at[2, 1]),
        pltpu.make_async_copy(ce_hbm, CI.at[0], in_sem.at[2, 2]),
        pltpu.make_async_copy(cn_hbm, CI.at[1], in_sem.at[2, 3]),
    ]
    for copy in geo_loads:
        copy.start()
    for c in range(ncat):
        load_mass(c).start()
        load_tracer(c).start()

    def remote(src, dst, send, recv, to):
        return pltpu.make_async_remote_copy(src_ref=src, dst_ref=dst, send_sem=send, recv_sem=recv, device_id=to, device_id_type=MESH)

    def y_south(k, c):
        return remote(ystage.at[k, c, 0], yrecv.at[k, c, 1], ys_sem.at[k, c, 0], yr_sem.at[k, c, 1], south)

    def y_north(k, c):
        return remote(ystage.at[k, c, 1], yrecv.at[k, c, north_slot], ys_sem.at[k, c, 1], yr_sem.at[k, c, north_slot], north)

    def y_from(k, c, slot):
        return remote(ystage.at[k, c, slot], yrecv.at[k, c, slot], ys_sem.at[k, c, slot], yr_sem.at[k, c, slot], north)

    def x_west(k, c):
        return remote(xsend.at[k, c], xrecv.at[k, c, 1], xs_sem.at[k, c, 0], xr_sem.at[k, c, 1], west)

    def x_east(k, c):
        return remote(xsend.at[k, c], xrecv.at[k, c, 0], xs_sem.at[k, c, 1], xr_sem.at[k, c, 0], east)

    g_north = remote(gystage, gyrecv, g_sem.at[0], g_sem.at[1], north)
    g_east = remote(gxsend, gxrecv, g_sem.at[2], g_sem.at[3], east)

    def send_y(k, c):
        for f in range(NF):
            ystage[k, c, 0, pl.ds(2 * f, 2)] = F[k][c, f, pl.ds(BASE, 2)]
            ystage[k, c, 1, pl.ds(2 * f, 2)] = F[k][c, f, pl.ds(BASE + height - 2, 2)]

        @pl.when(top)
        def _():
            wide = (2 * NF, breadth)
            back = breadth - 1 - lax.broadcasted_iota(jnp.int32, wide, 1)
            row = lax.broadcasted_iota(jnp.int32, wide, 0)
            edge = jnp.take_along_axis(ystage[k, c, 1], back, axis=1)
            ystage[k, c, 1] = pick(lax.rem(row, 2) == 0, pltpu.roll(edge, 2 * NF - 1, 0), pltpu.roll(edge, 1, 0))

        @pl.when(inner)
        def _():
            y_south(k, c).start()

        y_north(k, c).start()

    def packed(values):
        found = pltpu.roll(values[0], 2, 1)
        for f in range(1, len(values)):
            found = pick(lane >= 4 * f, pltpu.roll(values[f], 2 + 4 * f, 1), found)
        return found

    def pack(source, target, fields, first, count):
        def tile(t, carry):
            at = first + 8 * t
            target[pl.ds(2 + at, 8)] = packed([source(f)[pl.ds(BASE + at, 8)] for f in range(fields)])
            return carry

        lax.fori_loop(0, count, tile, 0, unroll=4 if count % 4 == 0 else 3)

    def pack_rim(k, c):
        for at in (-2, height - 6):
            xsend[k, c, pl.ds(2 + at, 8)] = packed([F[k][c, f, pl.ds(BASE + at, 8)] for f in range(NF)])

    def send_x(k, c):
        y_from(k, c, 1).wait_recv()
        for f in range(NF):
            F[k][c, f, pl.ds(BASE + height, 2)] = yrecv[k, c, 1, pl.ds(2 * f, 2)]

        @pl.when(inner)
        def _():
            y_from(k, c, 0).wait_recv()
            for f in range(NF):
                F[k][c, f, pl.ds(BASE - 2, 2)] = yrecv[k, c, 0, pl.ds(2 * f, 2)]

        @pl.when(bottom)
        def _():
            for f in range(NF):
                F[k][c, f, pl.ds(BASE - 2, 2)] = jnp.zeros((2, breadth), jnp.float32)

        pack_rim(k, c)
        x_west(k, c).start()
        x_east(k, c).start()

    for copy in geo_loads:
        copy.wait()
    GF[2, inside] = CI[0].astype(jnp.float32)
    GF[3, inside] = CI[1].astype(jnp.float32)
    for f in range(4):
        gystage[pl.ds(f, 1)] = GF[f, pl.ds(BASE + height - 1, 1)]

    @pl.when(inner)
    def _():
        pl.semaphore_wait(barrier, 4)

    @pl.when(bottom)
    def _():
        pl.semaphore_wait(barrier, 3)

    @pl.when(jnp.logical_not(top))
    def _():
        g_north.start()

    block_rows = height // ice.shape[0]
    block_cols = breadth // ice.shape[1]

    def first(c, carry):
        load_mass(c).wait()
        load_tracer(c).wait()
        for r in range(ice.shape[0]):
            mask = jnp.zeros((block_rows, breadth), jnp.float32)
            wide = lax.broadcasted_iota(jnp.int32, (block_rows, breadth), 1)
            for q in range(ice.shape[1]):
                mask = pick(wide >= q * block_cols, ice[r, q].astype(jnp.float32), mask)
            band = pl.ds(BASE + r * block_rows, block_rows)
            FA[c, 0, band] = FA[c, 0, band] * mask
        send_y(0, c)
        return carry

    lax.fori_loop(0, ncat, first, 0)

    def columns(c, carry):
        pack(lambda f: FA.at[c, f], xsend.at[0, c], NF, 0, tiles)
        return carry

    lax.fori_loop(0, ncat, columns, 0)

    @pl.when(inner)
    def _():
        g_north.wait_recv()
        for f in range(4):
            GF[f, pl.ds(BASE - 1, 1)] = gyrecv[pl.ds(f, 1)]

    @pl.when(bottom)
    def _():
        for f in range(4):
            GF[f, pl.ds(BASE - 1, 1)] = jnp.zeros((1, breadth), jnp.float32)

    pack(lambda f: GF.at[f], gxsend, 4, -2, tiles + 1)
    g_east.start()

    def second(c, carry):
        send_x(0, c)
        return carry

    lax.fori_loop(0, ncat, second, 0)


    def save(where, at, values):
        for q, value in enumerate(values):
            where[q, at] = value

    def from_west(x, packed, f):
        return pltpu.roll(pick(lane == breadth - 1, pltpu.roll(packed, (breadth - 2 - 4 * f) % breadth, 1), x), 1, 1)

    def geometry(t, carry):
        here = pl.ds(pl.multiple_of(BASE + 8 * t, 8), 8)
        below = pl.ds(BASE - 1 + 8 * t, 8)
        at = pl.ds(pl.multiple_of(8 * t, 8), 8)
        u, v = GF[0, here], GF[1, here]
        u_below, v_below = GF[0, below], GF[1, below]
        save(GE, at, edge_geometry(0.5 * (u + u_below), jnp.abs(v_below), jnp.abs(v), GF[2, here]))
        return carry

    lax.fori_loop(0, tiles, geometry, 0, unroll=2)
    g_east.wait_recv()

    def west_geometry(t, carry):
        here = pl.ds(pl.multiple_of(BASE + 8 * t, 8), 8)
        below = pl.ds(BASE - 1 + 8 * t, 8)
        at = pl.ds(pl.multiple_of(8 * t, 8), 8)
        u, v = GF[0, here], GF[1, here]
        u_below, v_below = GF[0, below], GF[1, below]
        mine, lower = gxrecv[pl.ds(2 + 8 * t, 8)], gxrecv[pl.ds(1 + 8 * t, 8)]
        u, u_below = from_west(u, mine, 0), from_west(u_below, lower, 0)
        v, v_below = from_west(v, mine, 1), from_west(v_below, lower, 1)
        save(GW, at, edge_geometry(0.5 * (u + u_below), jnp.abs(v_below), jnp.abs(v), from_west(GF[2, here], mine, 2)))
        return carry

    lax.fori_loop(0, tiles, west_geometry, 0, unroll=2)

    def north_geometry(t, carry):
        start = jnp.minimum(8 * t - 1, height - 8)
        here = pl.ds(BASE + start, 8)
        u, v, packed = GF[0, here], GF[1, here], gxrecv[pl.ds(2 + start, 8)]

        u_west, v_west = from_west(u, packed, 0), from_west(v, packed, 1)
        save(GN, here, edge_geometry(0.5 * (v + v_west), jnp.abs(u_west), jnp.abs(u), GF[3, here]))
        return carry

    lax.fori_loop(0, tiles + 1, north_geometry, 0, unroll=3)

    def edges(where, at):
        a, area, x1, x2, off, case = (where[q, at] for q in range(6))
        return a, area, x1, x2, off, a > 0.0, case == 2.0

    edge_lanes = (lane >= breadth - 2, lane >= breadth - 1, lane < 1, lane < 2)
    left = lax.rem(lane, 4) < 2

    def shift_tile(k, c, S, t):
        at = pl.ds(8 * t if isinstance(t, int) else pl.multiple_of(8 * t, 8), 8)
        halo = pick(left, xrecv[k, c, 0, at], xrecv[k, c, 1, at])

        def piece(f):
            value = F[k][c, f, pl.ds(BASE - 2 + 8 * t, 8)]
            side = pltpu.roll(halo, (breadth - 2 - 4 * f) % breadth, 1)
            for q, shift in enumerate(SHIFTS):
                S[q, f, at] = pltpu.roll(pick(edge_lanes[q], side, value), -shift % breadth, 1)

        return [functools.partial(piece, f) for f in range(NF)]

    def advance(k, c, S, ahead):
        def reader(f, start):
            def get(row, col):
                if col == 0:
                    return F[k][c, f, pl.ds(BASE + start + row, 8)]
                return S[SHIFTS.index(col), f, pl.ds(2 + start + row, 8)]

            return remember(get)

        def north_edges(get, start):
            at = pl.ds(BASE + start, 8)
            flux, points = mass_flux(get, edges(GN, at))
            ND[0, at] = flux
            for q, (value, _) in enumerate(points.values()):
                ND[1 + q, at] = value
            return flux, points

        north_edges(reader(0, -1), -1)
        for work in ahead(tiles):
            work()

        def tile(t, carry):
            start = pl.multiple_of(8 * t, 8)
            at = pl.ds(start, 8)
            after = pl.ds(BASE + start, 8)
            before = pl.ds(BASE - 1 + start, 8)
            work = ahead(t)
            get = reader(0, start)
            mass = get(0, 0)
            north, north_points = north_edges(get, start)
            if work:
                work[0]()
            east, east_points = mass_flux(lambda n, t: get(t, n), edges(GE, at))
            west, west_points = mass_flux(lambda n, t: get(t, n - 1), edges(GW, at))
            total = {(0, 0): mass}

            def emit(f, value):
                if k + 1 < STEPS:
                    F[k + 1][c, f, after] = value
                elif f:
                    tracer_out[c, f - 1, at] = value
                else:
                    mass_out[c, at] = value


            def add(where, value, sign):
                if where not in total:
                    total[where] = value if sign > 0 else -value
                elif sign > 0:
                    total[where] = total[where] + value
                else:
                    total[where] = total[where] - value

            for (n, q), (value, sign) in west_points.items():
                add((q, n - 1), value, sign)
            for i, ((n, q), (_, sign)) in enumerate(north_points.items()):
                add((n - 1, q), ND[1 + i, before], sign)
            for (n, q), (value, sign) in east_points.items():
                add((q, n), value, -sign)
            for (n, q), (value, sign) in north_points.items():
                add((n, q), value, -sign)
            new_mass = mass - (east - west) - (north - ND[0, before])
            emit(0, new_mass)
            scale = 1.0 / jnp.maximum(new_mass, FLOOR)
            for f in range(1, NF):
                if work:
                    work[f]()
                get = reader(f, start)
                sums = [None, None]
                for i, ((row, col), value) in enumerate(total.items()):
                    term = value * get(row, col)
                    sums[i % 2] = term if sums[i % 2] is None else sums[i % 2] + term
                emit(f, (sums[0] + sums[1]) * scale)
            return carry

        if k + 1 < STEPS:
            north_edges(reader(0, height - 9), height - 9)
            lax.fori_loop(0, 2, lambda i, carry: tile((tiles - 1) * i, carry), 0, unroll=2)
            send_y(k + 1, c)
            lax.fori_loop(1, tiles - 1, tile, 0, unroll=3)
        else:
            lax.fori_loop(0, tiles, tile, 0, unroll=1 if ahead(0) else 4)

    def x_wait(k, c):
        x_east(k, c).wait_recv()
        x_west(k, c).wait_recv()

    order = [(k, c) for k in range(STEPS) for c in range(ncat)]
    x_wait(0, 0)

    def whole(t, carry):
        for work in shift_tile(0, 0, SA, t):
            work()
        return carry

    lax.fori_loop(0, tiles + 1, whole, 0, unroll=3)
    for i, (k, c) in enumerate(order):
        if False:
            x_wait(*order[i + 1])
            ahead = functools.partial(shift_tile, *order[i + 1], (SA, SB)[(i + 1) % 2])
        else:
            ahead = lambda t: []
        advance(k, c, (SA, SB)[i % 2], ahead)
        if 2 <= i < ncat + 2:
            send_x(1, i - 2)
        if i + 1 < len(order):
            x_wait(*order[i + 1])
            nxt = order[i + 1]

            def whole(t, carry, nxt=nxt, S=(SA, SB)[(i + 1) % 2]):
                for work in shift_tile(*nxt, S, t):
                    work()
                return carry

            lax.fori_loop(0, tiles + 1, whole, 0, unroll=3)
        if k == 0:
            pack(lambda f: FB.at[c, f], xsend.at[1, c], NF, 0, tiles)

    @pl.when(jnp.logical_not(top))
    def _():
        g_north.wait_send()

    g_east.wait_send()

    def finish(c, carry):
        for k in range(STEPS):
            @pl.when(inner)
            def _():
                y_south(k, c).wait_send()

            y_north(k, c).wait_send()
            x_west(k, c).wait_send()
            x_east(k, c).wait_send()
        return carry

    lax.fori_loop(0, ncat, finish, 0)


def solution(mesh):
    nx, ny = mesh.shape["gx"], mesh.shape["gy"]

    def per_device(mass, tracer, uvel, vvel, case_east, case_north, ice):
        ncat, height, breadth = mass.shape
        rows = height + 2 * BASE
        packed = height + 8
        f32 = jnp.float32
        hbm = pl.BlockSpec(memory_space=pl.ANY)
        return pl.pallas_call(
            functools.partial(kernel, nx, ny, ncat, height, breadth),
            out_shape=(pltpu.VMEM(mass.shape, f32), pltpu.VMEM(tracer.shape, f32)),
            in_specs=[hbm] * 6 + [pl.BlockSpec(memory_space=pltpu.SMEM)],
            out_specs=(pl.BlockSpec(memory_space=pltpu.VMEM),) * 2,
            scratch_shapes=[
                pltpu.VMEM((ncat, NF, rows, breadth), f32),
                pltpu.VMEM((ncat, NF, rows, breadth), f32),
                pltpu.VMEM((4, NF, packed, breadth), f32),
                pltpu.VMEM((4, NF, packed, breadth), f32),
                pltpu.VMEM((17, packed, breadth), f32),
                pltpu.VMEM((4, rows, breadth), f32),
                pltpu.VMEM((2, height, breadth), jnp.int32),
                pltpu.VMEM((6, height, breadth), f32),
                pltpu.VMEM((6, packed, breadth), f32),
                pltpu.VMEM((6, height, breadth), f32),
                pltpu.VMEM((STEPS, ncat, 2, 2 * NF, breadth), f32),
                pltpu.VMEM((STEPS, ncat, 2, 2 * NF, breadth), f32),
                pltpu.VMEM((STEPS, ncat, packed, breadth), f32),
                pltpu.VMEM((STEPS, ncat, 2, packed, breadth), f32),
                pltpu.VMEM((8, breadth), f32),
                pltpu.VMEM((8, breadth), f32),
                pltpu.VMEM((packed, breadth), f32),
                pltpu.VMEM((packed, breadth), f32),
                pltpu.SemaphoreType.DMA((3, max(ncat, 4))),
                pltpu.SemaphoreType.DMA((STEPS, ncat, 2)),
                pltpu.SemaphoreType.DMA((STEPS, ncat, 2)),
                pltpu.SemaphoreType.DMA((STEPS, ncat, 2)),
                pltpu.SemaphoreType.DMA((STEPS, ncat, 2)),
                pltpu.SemaphoreType.DMA((4,)),
            ],
            compiler_params=pltpu.CompilerParams(collective_id=0, has_side_effects=True),
        )(mass, tracer, uvel, vvel, case_east, case_north, ice)

    placed = (P(None, "gy", "gx"), P(None, None, "gy", "gx")) + (P("gy", "gx"),) * 5
    return jax.shard_map(
        per_device,
        mesh=mesh,
        in_specs=placed,
        out_specs=(P(None, "gy", "gx"), P(None, None, "gy", "gx")),
        check_vma=False,
    )
```
